32 devices in a mesh: fsdp: 4 (over z), dp: 2 (over y), tensor: 4 (over x, core).
Axes of the slice: x: 2, y: 2, z: 4, core: 2. Of those that a mesh axis runs over, the one named last changes fastest.
Arguments:
- tokens: bfloat16 [2048, 7168], P(('fsdp', 'dp')), may hold values from -6 to 6
- panels: bfloat16 [112, 4, 128, 128], P('tensor', None, 'fsdp'), may hold values from -0.25 to 0.25
- block_rows: int32 [112, 4], P('tensor'), may hold values from 0 to 55, as said below
- low_in: bfloat16 [7168, 512], P('tensor'), may hold values from -0.0625 to 0.0625
- low_out: bfloat16 [112, 4, 128, 128], P('tensor'), may hold values from -0.25 to 0.25
- cotangent: bfloat16 [2048, 14336], P(('fsdp', 'dp'), 'tensor'), may hold values from -0.125 to 0.125
Outputs:
- activated: bfloat16 [2048, 14336], P(('fsdp', 'dp'), 'tensor')
- panel_grad: float32 [112, 4, 128, 128], P('tensor', None, 'fsdp')
The draws below stay inside these ranges and needn't reach their ends.
Inputs may be any that keep to these rules, and one draw needn't show every extreme that they name: `block_rows`: each column block c names 4 distinct row blocks, the first of them c modulo 56.
All inputs are finite; a program needn't handle non-finite values.
Results may differ from the reference program's by a relative error of at most 0.0039.
Values may be sent and summed in bfloat16 or wider, within the bound.
A program may use at most 128 MiB of HBM per device.

```python
import jax
import jax.numpy as jnp
from jax import lax

D = 7168
FF = 14336
BLK = 128
K = 4
R = 512
RB = 56
CB = 112
RBLK = 4
TOKENS = 2048


def draw_block_rows(key, part):
    scores = jax.random.randint(key, (CB, RB), 0, 1 << 20)
    column = lax.broadcasted_iota(jnp.int32, (CB, RB), 0)
    within = lax.broadcasted_iota(jnp.int32, (CB, RB), 1)
    scores = scores * RB + within
    scores = jnp.where(within == column % RB, -1, scores)
    ranking = jnp.argsort(scores, axis=1, stable=True)
    return ranking[:, :K].astype(jnp.int32)


def steps_of(key, shape, cuts, smallest, high):
    def one(axis_at, shards_of):
        heights = jax.random.uniform(jax.random.fold_in(jax.random.fold_in(key, 6), axis_at), (shards_of,), jnp.float32, smallest / len(cuts), high / len(cuts))
        return jnp.repeat(jnp.exp(heights), shape[axis_at] // shards_of).reshape((-1,) + (1,) * (len(shape) - axis_at - 1))

    gain = one(*cuts[0])
    for cut in cuts[1:]:
        gain = gain * one(*cut)
    return gain


def scatter_about(key, extent, width, bound, cuts=(), dtype=jnp.bfloat16):
    loudness = steps_of(key, extent, cuts, -0.22, 0.18) if cuts else 1.0
    drawn = jax.random.normal(key, extent, jnp.float32) * width * loudness
    return jnp.minimum(jnp.maximum(drawn, -bound), bound).astype(dtype)


def setup_inputs(seed: int = 0) -> dict:
    splits = jax.random.split(jax.random.key(seed), 7)
    tokens = scatter_about(splits[0], (TOKENS, D), 1.0, 6.0, ((0, 8),))
    panels = scatter_about(splits[1], (CB, K, BLK, BLK), (K * BLK) ** -0.5, 0.25, ((0, 4), (2, 4)))
    block_rows = draw_block_rows(jax.random.fold_in(splits[6], 71), 0)
    low_in = scatter_about(splits[3], (D, R), D ** -0.5, 0.0625, ((0, 4),))
    low_out = scatter_about(splits[4], (CB, RBLK, BLK, BLK), R ** -0.5, 0.25, ((0, 4),))
    cotangent = scatter_about(splits[5], (TOKENS, FF), TOKENS ** -0.5, 0.125, ((0, 8), (1, 4)))
    return {"tokens": tokens, "panels": panels, "block_rows": block_rows, "low_in": low_in, "low_out": low_out, "cotangent": cotangent}


def activate(values):
    return jax.nn.gelu(values, approximate=True)

def reference(tokens, panels, block_rows, low_in, low_out, cotangent):
    latent = jnp.dot(tokens, low_in, preferred_element_type=jnp.float32).astype(jnp.bfloat16)
    latent_tiles = latent.reshape(TOKENS, RBLK, BLK).astype(jnp.float32)
    tiled_rows = tokens.reshape(TOKENS, RB, BLK)
    slopes_in = jnp.transpose(cotangent.reshape(TOKENS, CB, BLK), (1, 0, 2))

    def one_column(inputs):
        rows_here, panel_here, lowout_here, slope_in = inputs
        picked = jnp.take(tiled_rows, rows_here.astype(jnp.int32), axis=1).astype(jnp.float32)
        low_part = jnp.einsum('tjr,jro->to', latent_tiles, lowout_here.astype(jnp.float32))
        sparse_part = jnp.einsum('tkr,kro->to', picked, panel_here.astype(jnp.float32))
        pre = low_part + sparse_part
        result, pullback = jax.vjp(activate, pre)
        slope = pullback(slope_in.astype(jnp.float32))[0].astype(jnp.bfloat16)
        grad_here = jnp.einsum('tkr,to->kro', picked, slope.astype(jnp.float32))
        return (result.astype(jnp.bfloat16), grad_here)
    outputs, panel_grad = lax.map(one_column, (block_rows, panels, low_out, slopes_in))
    activated = jnp.transpose(outputs, (1, 0, 2)).reshape(TOKENS, FF)
    return (activated, panel_grad)
```

```python
import functools
import math

import jax
import jax.numpy as jnp
from jax import lax
from jax.experimental import pallas as pl
from jax.experimental.pallas import tpu as pltpu
from jax.sharding import PartitionSpec as P

MESH = pl.DeviceIdType.MESH
GELU_SCALE = math.sqrt(2.0 / math.pi)
GELU_CUBIC = 0.044715
COLS = 2
AHEAD = 3
AHEAD_END = 5
GATHER_LAG = 2
ACROSS_LAG = 2
EARLY_LAG = 2
SUM_LAG = 2
FINAL_LAG = 2
GATHER_CUT = 6
PIECES = 1
SUM_CUT = 4
LATENT_AT = (1, 3)


def kernel(
    nz, ny, nt, per, rows, size, cuts,
    tokens_hbm, panels_hbm, rows_hbm, low_in_hbm, low_out_hbm, cot_hbm,
    act_ref, grad_ref,
    rows_ref, tok, lin, lout, cot, pan, own, sbuf, rbuf, ysend, yrecv, xsend, xrecv,
    lpart, lrecv, lat,
    local_sem, tok_sem, ag_send, ag_recv, ay_send, ay_recv, rs_send, rs_recv,
    y_send, y_recv, x_send, x_recv, l1_send, l1_recv, l2_send, l2_recv,
):
    z, y, t = lax.axis_index("fsdp"), lax.axis_index("dp"), lax.axis_index("tensor")
    height, blk = panels_hbm.shape
    chunks = height // size
    deep = per * rows
    nc = size // deep
    gcut, scut = cuts
    gwide, swide = size - (ny - 1) * gcut, size - (ny - 1) * scut
    f32 = jnp.float32

    barrier = pltpu.get_barrier_semaphore()

    @pl.when(z > 0)
    def _():
        pl.semaphore_signal(barrier, inc=1, device_id={"fsdp": z - 1}, device_id_type=MESH)

    @pl.when(z < nz - 1)
    def _():
        pl.semaphore_signal(barrier, inc=1, device_id={"fsdp": z + 1}, device_id_type=MESH)

    for i in range(1, nt):
        pl.semaphore_signal(
            barrier, inc=1, device_id={"tensor": lax.rem(t + i, nt)}, device_id_type=MESH)
    for i in range(1, ny):
        pl.semaphore_signal(
            barrier, inc=1, device_id={"dp": lax.rem(y + i, ny)}, device_id_type=MESH)

    in_copies = [
        pltpu.make_async_copy(src, dst, local_sem.at[i])
        for i, (src, dst) in enumerate(
            [(low_in_hbm, lin), (panels_hbm, pan.at[z]), (low_out_hbm, lout), (cot_hbm, cot),
             (rows_hbm, rows_ref)]
        )
    ]
    feature_blocks, toks = tok.shape[:2]

    def token_copy(b):
        return pltpu.make_async_copy(
            tokens_hbm.at[:, pl.ds(pl.multiple_of(b * blk, blk), blk)], tok.at[b], tok_sem.at[b])

    def token_start(b, carry):
        token_copy(b).start()
        return carry

    def token_wait(b, carry):
        token_copy(b).wait()
        return carry

    neighbours = jnp.where(z > 0, 1, 0) + jnp.where(z < nz - 1, 1, 0)
    pl.semaphore_wait(barrier, nt - 1 + ny - 1 + neighbours)

    def reach(j, cut):
        return pl.ds(pl.multiple_of(j * size + y * cut, 8), size - (ny - 1) * cut)

    def alone(j, p, cut):
        first = p * ((size - cut) // max(ny - 1, 1))
        return pl.ds(pl.multiple_of(j * size + first, 8), cut)

    def gather_copy(way, shard, j, from_input=False):
        there = z + 1 if way == 0 else z - 1
        at = reach(j, gcut)
        return pltpu.make_async_remote_copy(
            src_ref=panels_hbm.at[at] if from_input else pan.at[shard, at],
            dst_ref=pan.at[shard, at],
            send_sem=ag_send.at[way, shard], recv_sem=ag_recv.at[shard, j],
            device_id={"fsdp": there}, device_id_type=MESH)

    def across_copy(i, shard, j):
        at = alone(j, y, gcut)
        return pltpu.make_async_remote_copy(
            src_ref=pan.at[shard, at], dst_ref=pan.at[shard, at],
            send_sem=ay_send.at[shard], recv_sem=ay_recv.at[i, j],
            device_id={"dp": lax.rem(y + i, ny)}, device_id_type=MESH)

    def send_own(way, j):
        pl.when(j < chunks)(lambda: gather_copy(way, z, j, True).start())

    def inside(j):
        return jnp.logical_and(j >= 0, j < chunks)

    up_ahead = jnp.where(z == 0, AHEAD_END, AHEAD)
    down_ahead = jnp.where(z == nz - 1, AHEAD_END, AHEAD)

    def first_own(j, carry):
        pl.when(jnp.logical_and(z < nz - 1, j < up_ahead))(lambda: send_own(0, j))
        pl.when(jnp.logical_and(z > 0, j < down_ahead))(lambda: send_own(1, j))
        return carry

    lax.fori_loop(0, max(AHEAD, AHEAD_END), first_own, 0)

    in_copies[0].start()
    lax.fori_loop(0, feature_blocks, token_start, 0)
    for copy in in_copies[1:]:
        copy.start()

    def pass_on(h, tau):
        j = tau - (h - 1) * GATHER_LAG

        def arrived(way, shard, more):
            gather_copy(way, shard, j).wait_recv()

            @pl.when(more)
            def _():
                gather_copy(way, shard, j).start()

            if gcut:
                for i in range(1, ny):
                    across_copy(i, shard, j).start()

        @pl.when(jnp.logical_and(inside(j), z - h >= 0))
        def _():
            arrived(0, z - h, z < nz - 1)

        @pl.when(jnp.logical_and(inside(j), z + h < nz))
        def _():
            arrived(1, z + h, z > 0)

    def across_done(j):
        if gcut:
            for i in range(1, ny):
                pltpu.make_async_copy(
                    pan.at[pl.ds(0, nz - 1), pl.ds(0, gcut)],
                    pan.at[pl.ds(0, nz - 1), pl.ds(0, gcut)], ay_recv.at[i, j]).wait()

    def lat_one(i):
        peer = lax.rem(t + i, nt)
        return pltpu.make_async_remote_copy(
            src_ref=lpart.at[peer], dst_ref=lrecv.at[i],
            send_sem=l1_send.at[i], recv_sem=l1_recv.at[i],
            device_id={"tensor": peer}, device_id_type=MESH)

    def lat_two(i, shard):
        peer = lax.rem(t + i, nt)
        return pltpu.make_async_remote_copy(
            src_ref=lat.at[shard], dst_ref=lat.at[shard],
            send_sem=l2_send.at[i], recv_sem=l2_recv.at[i],
            device_id={"tensor": peer}, device_id_type=MESH)

    def latent_part():
        in_copies[0].wait()
        lax.fori_loop(0, feature_blocks, token_wait, 0)
        blocks = lin.shape[0] // blk
        lpart[...] = jnp.dot(
            jnp.concatenate([tok[t * blocks + b] for b in range(blocks)], axis=1), lin[...],
            preferred_element_type=f32,
        ).reshape(lpart.shape)
        for i in range(1, nt):
            lat_one(i).start()

    def latent_sum():
        total = lpart[t]
        for i in range(1, nt):
            lat_one(i).wait_recv()
            total = total + lrecv[i]
        lat[t] = total.astype(lat.dtype)
        for i in range(1, nt):
            lat_two(i, t).start()
        for copy in in_copies[1:]:
            copy.wait()

    def latent_done():
        for i in range(1, nt):
            lat_two(i, lax.rem(t + nt - i, nt)).wait_recv()

    def column(c):
        picked = jnp.concatenate([tok[rows_ref[k, c]] for k in range(per)], axis=1)
        lines = pl.ds(pl.multiple_of(c * deep, 8), deep)
        parts = [pan[s, lines] for s in range(nz)]
        weight = jnp.concatenate(
            [parts[s][k * rows:(k + 1) * rows] for k in range(per) for s in range(nz)], axis=0)
        latent = lat[...].reshape(toks, -1)
        pre = jnp.dot(latent, lout[c], preferred_element_type=f32)
        pre = pre + jnp.dot(picked, weight, preferred_element_type=f32)
        at = pl.ds(pl.multiple_of(c * blk, blk), blk)
        square = pre * pre
        curve = jnp.tanh(GELU_SCALE * (pre + GELU_CUBIC * (square * pre)))
        half = 0.5 * (1.0 + curve)
        act_ref[:, at] = (pre * half).astype(act_ref.dtype)
        inner = GELU_SCALE * (1.0 + 3.0 * GELU_CUBIC * square)
        deriv = half + 0.5 * pre * (1.0 - curve * curve) * inner
        slope = (cot[:, at].astype(f32) * deriv).astype(jnp.bfloat16)
        grad = lax.dot_general(
            picked, slope, (((0,), (0,)), ((), ())), preferred_element_type=f32)
        for d in range(nz):
            own[d, lines] = jnp.concatenate(
                [grad[k * blk + d * rows:k * blk + (d + 1) * rows] for k in range(per)], axis=0)

    def early_copy(i, j):
        peer = lax.rem(y + i, ny)
        return pltpu.make_async_remote_copy(
            src_ref=xsend.at[:, alone(j, peer, scut)],
            dst_ref=xrecv.at[i - 1, :, pl.ds(pl.multiple_of(j * scut, 8), scut)],
            send_sem=x_send.at[i], recv_sem=x_recv.at[i, j],
            device_id={"dp": peer}, device_id_type=MESH)

    def early_start(j):
        if scut:
            for i in range(1, ny):
                at = alone(j, lax.rem(y + i, ny), scut)
                xsend[:, at] = own[:, at].astype(xsend.dtype)
                early_copy(i, j).start()

    def early_done(j):
        if scut:
            at = alone(j, y, scut)
            total = own[:, at]
            for i in range(1, ny):
                early_copy(i, j).wait_recv()
                total = total + xrecv[i - 1, :, pl.ds(pl.multiple_of(j * scut, 8), scut)].astype(f32)
            own[:, at] = total

    def sum_copy(way, d, j):
        there = z + 1 if way == 0 else z - 1
        at = reach(j, scut)
        return pltpu.make_async_remote_copy(
            src_ref=sbuf.at[d, at], dst_ref=rbuf.at[way, d, at],
            send_sem=rs_send.at[d], recv_sem=rs_recv.at[way, d, j],
            device_id={"fsdp": there}, device_id_type=MESH)

    def flow(way, d, j, first):
        at = reach(j, scut)

        @pl.when(first)
        def _():
            sbuf[d, at] = own[d, at].astype(sbuf.dtype)

        @pl.when(jnp.logical_not(first))
        def _():
            sum_copy(way, d, j).wait_recv()
            sbuf[d, at] = (own[d, at] + rbuf[way, d, at].astype(f32)).astype(sbuf.dtype)

        sum_copy(way, d, j).start()

    def final_copy(i, j):
        at = reach(j, scut)
        return pltpu.make_async_remote_copy(
            src_ref=ysend.at[at], dst_ref=yrecv.at[i - 1, at],
            send_sem=y_send.at[i], recv_sem=y_recv.at[i, j],
            device_id={"dp": lax.rem(y + i, ny)}, device_id_type=MESH)

    def finish(j):
        at = reach(j, scut)

        def landed(way):
            sum_copy(way, z, j).wait_recv()
            return rbuf[way, z, at].astype(f32)

        @pl.when(z == 0)
        def _():
            ysend[at] = (own[z, at] + landed(1)).astype(ysend.dtype)

        @pl.when(z == nz - 1)
        def _():
            ysend[at] = (own[z, at] + landed(0)).astype(ysend.dtype)

        @pl.when(jnp.logical_and(z > 0, z < nz - 1))
        def _():
            ysend[at] = (own[z, at] + landed(0) + landed(1)).astype(ysend.dtype)

        for i in range(1, ny):
            final_copy(i, j).start()

    def result(j):
        for i in range(1, ny):
            final_copy(i, j).wait_recv()
        if scut:
            mine = alone(j, y, scut)
            grad_ref[mine] = ysend[mine].astype(f32)
            for i in range(1, ny):
                there = alone(j, lax.rem(y + ny - i, ny), scut)
                grad_ref[there] = yrecv[i - 1, there].astype(f32)
        if size - ny * scut:
            shared = pl.ds(pl.multiple_of(j * size + (ny - 1) * scut, 8), size - ny * scut)
            value = ysend[shared].astype(f32)
            for i in range(1, ny):
                value = value + yrecv[i - 1, shared].astype(f32)
            grad_ref[shared] = value

    compute_at = (nz - 2) * GATHER_LAG + ACROSS_LAG
    sum_at = compute_at + EARLY_LAG
    finish_at = sum_at + (nz - 1) * SUM_LAG
    steps = chunks + finish_at + FINAL_LAG

    def step(tau, carry):
        def hop(k, carry):
            pass_on(nz - 1 - k, tau)
            return carry

        lax.fori_loop(0, nz - 1, hop, 0)
        pl.when(z < nz - 1)(lambda: send_own(0, tau + up_ahead))
        pl.when(z > 0)(lambda: send_own(1, tau + down_ahead))

        summed = tau - sum_at
        pl.when(inside(summed))(lambda: early_done(summed))
        up, down = summed - z * SUM_LAG, summed - (nz - 1 - z) * SUM_LAG

        def towards(d, carry):
            far = nz - 1 - d

            @pl.when(jnp.logical_and(far > z, inside(up)))
            def _():
                flow(0, far, up, z == 0)

            @pl.when(jnp.logical_and(d < z, inside(down)))
            def _():
                flow(1, d, down, z == nz - 1)

            return carry

        lax.fori_loop(0, nz, towards, 0)
        last = tau - finish_at
        pl.when(inside(last))(lambda: finish(last))
        done = last - FINAL_LAG
        pl.when(inside(done))(lambda: result(done))

        pl.when(tau == LATENT_AT[0])(latent_part)
        pl.when(tau == LATENT_AT[1])(latent_sum)
        pl.when(tau == compute_at)(latent_done)
        now = tau - compute_at

        @pl.when(inside(now))
        def _():
            across_done(now)
            for i in range(nc):
                column(now * nc + i)
            early_start(now)

        return carry

    lax.fori_loop(0, steps, step, 0)

    for i in range(1, nt):
        lat_one(i).wait_send()
        lat_two(i, t).wait_send()

    def gather_left(way, s):
        at = pan.at[s, pl.ds(0, chunks * gwide)]
        pltpu.make_async_copy(at, at, ag_send.at[way, s]).wait()

    def left(s, carry):
        @pl.when(jnp.logical_and(s <= z, z < nz - 1))
        def _():
            gather_left(0, s)

        @pl.when(jnp.logical_and(s >= z, z > 0))
        def _():
            gather_left(1, s)

        @pl.when(s != z)
        def _():
            if gcut:
                at = pan.at[s, pl.ds(0, chunks * gcut)]
                for i in range(1, ny):
                    pltpu.make_async_copy(at, at, ay_send.at[s]).wait()
            at = sbuf.at[s, pl.ds(0, chunks * swide)]
            pltpu.make_async_copy(at, at, rs_send.at[s]).wait()

        return carry

    lax.fori_loop(0, nz, left, 0)
    for i in range(1, ny):
        at = ysend.at[pl.ds(0, chunks * swide)]
        pltpu.make_async_copy(at, at, y_send.at[i]).wait()
        if scut:
            at = xsend.at[:, pl.ds(0, chunks * scut)]
            pltpu.make_async_copy(at, at, x_send.at[i]).wait()


def write_out(act_in, grad_in, act_out, grad_out, sem):
    copies = []
    for a, (src, dst) in enumerate([(act_in, act_out), (grad_in, grad_out)]):
        step = src.shape[0] // PIECES
        for i in range(PIECES):
            at = pl.ds(i * step, step)
            copies.append(pltpu.make_async_copy(src.at[at], dst.at[at], sem.at[a, i]))
    for copy in copies:
        copy.start()
    for copy in copies:
        copy.wait()


def on_device(sizes, tokens, panels, block_rows, low_in, low_out, cotangent):
    nz, ny, nt = sizes
    cols, per, rows, blk = panels.shape
    toks, rank = tokens.shape[0], low_in.shape[1]
    nc = COLS if ny <= 2 and cols % COLS == 0 else 4 if cols % 4 == 0 else 1
    chunks = cols // nc
    size = nc * per * rows
    cuts = tuple(
        0 if ny == 1 else size // ny if ny > 2 else max(16, size * cut // 16 // 16 * 16)
        for cut in (GATHER_CUT, SUM_CUT))
    bf16, f32 = jnp.bfloat16, jnp.float32
    hop_type = bf16 if nz <= 4 and ny <= 2 else f32
    low_out = low_out.reshape(cols, rank, blk)
    lines = panels.reshape(cols * per * rows, blk)
    height = lines.shape[0]
    hbm = pl.BlockSpec(memory_space=pl.ANY)
    vmem = pl.BlockSpec(memory_space=pltpu.VMEM)
    dma = pltpu.SemaphoreType.DMA
    others = max(ny - 1, 1)
    activated, grad = pl.pallas_call(
        functools.partial(kernel, nz, ny, nt, per, rows, size, cuts),
        out_shape=(
            pltpu.VMEM(cotangent.shape, bf16),
            pltpu.VMEM(lines.shape, f32),
        ),
        in_specs=[hbm] * 6,
        out_specs=(vmem, vmem),
        scratch_shapes=[
            pltpu.SMEM((per, cols), jnp.int32),
            pltpu.VMEM((tokens.shape[1] // blk, toks, blk), bf16),
            pltpu.VMEM(low_in.shape, bf16),
            pltpu.VMEM(low_out.shape, bf16),
            pltpu.VMEM(cotangent.shape, bf16),
            pltpu.VMEM((nz, height, blk), bf16),
            pltpu.VMEM((nz, height, blk), f32),
            pltpu.VMEM((nz, height, blk), hop_type),
            pltpu.VMEM((2, nz, height, blk), hop_type),
            pltpu.VMEM((height, blk), hop_type),
            pltpu.VMEM((others, height, blk), hop_type),
            pltpu.VMEM((nz, height, blk), hop_type),
            pltpu.VMEM((others, nz, max(chunks * cuts[1], 16), blk), hop_type),
            pltpu.VMEM((nt, toks // nt, rank), f32),
            pltpu.VMEM((nt, toks // nt, rank), f32),
            pltpu.VMEM((nt, toks // nt, rank), bf16),
            dma((5,)),
            dma((tokens.shape[1] // blk,)),
            dma((2, nz)),
            dma((nz, chunks)),
            dma((nz,)),
            dma((ny, chunks)),
            dma((nz,)),
            dma((2, nz, chunks)),
            dma((ny,)),
            dma((ny, chunks)),
            dma((ny,)),
            dma((ny, chunks)),
            dma((nt,)),
            dma((nt,)),
            dma((nt,)),
            dma((nt,)),
        ],
        compiler_params=pltpu.CompilerParams(
            collective_id=0, has_side_effects=True, vmem_limit_bytes=52 * 1024 * 1024),
    )(tokens, lines, block_rows.T, low_in, low_out, cotangent)
    activated, grad = pl.pallas_call(
        write_out,
        out_shape=(
            jax.ShapeDtypeStruct(cotangent.shape, bf16),
            jax.ShapeDtypeStruct(lines.shape, f32),
        ),
        in_specs=[vmem, vmem],
        out_specs=(hbm, hbm),
        scratch_shapes=[dma((2, PIECES))],
        compiler_params=pltpu.CompilerParams(vmem_limit_bytes=1024 * 1024),
    )(pltpu.with_memory_space_constraint(activated, pltpu.VMEM), pltpu.with_memory_space_constraint(grad, pltpu.VMEM))
    return activated, grad.reshape(panels.shape)


def solution(mesh):
    in_specs = (
        P(("fsdp", "dp"), None),
        P("tensor", None, "fsdp", None),
        P("tensor", None),
        P("tensor", None),
        P("tensor", None, None, None),
        P(("fsdp", "dp"), "tensor"),
    )
    out_specs = (P(("fsdp", "dp"), "tensor"), P("tensor", None, "fsdp", None))
    sizes = tuple(mesh.shape[name] for name in ("fsdp", "dp", "tensor"))
    return jax.shard_map(
        functools.partial(on_device, sizes),
        mesh=mesh, in_specs=in_specs, out_specs=out_specs, check_vma=False,
    )
```

```python
import functools
import math

import jax
import jax.numpy as jnp
from jax import lax
from jax.experimental import pallas as pl
from jax.experimental.pallas import tpu as pltpu
from jax.sharding import PartitionSpec as P

MESH = pl.DeviceIdType.MESH
GELU_SCALE = math.sqrt(2.0 / math.pi)
GELU_CUBIC = 0.044715
COLS = 2
AHEAD = 4
AHEAD_END = 10
GATHER_LAG = 2
ACROSS_LAG = 1
EARLY_LAG = 2
SUM_LAG = 3
FINAL_LAG = 3
GATHER_CUT = ((5, 8), (12, 5), (14, 0))
SUM_CUT = ((5, 4), (13, 5), (14, 6))
PIECES = 1
ORDER = "gslr"


def by_cut(plan, j, act):
    if len(plan) == 1:
        act(plan[0][2])
    else:
        for first, end, cut in plan:
            pl.when(jnp.logical_and(j >= first, j < end))(functools.partial(act, cut))


def kernel(
    nz, ny, nt, per, rows, size, gplan, splan,
    tokens_hbm, panels_hbm, rows_hbm, low_in_hbm, low_out_hbm, cot_hbm,
    act_ref, grad_ref,
    rows_ref, tok, lin, lout, cot, pan, own, sbuf, rbuf, ysend, yrecv, xsend, xrecv,
    lpart, lhalf, lpair, lrecv, lat,
    local_sem, tok_sem, ag_send, ag_recv, ay_send, ay_recv, rs_send, rs_recv,
    y_send, y_recv, x_send, x_recv, l0_send, l0_recv, l1_send, l1_recv, l2_send, l2_recv,
):
    z, y, t = lax.axis_index("fsdp"), lax.axis_index("dp"), lax.axis_index("tensor")
    height, blk = panels_hbm.shape
    chunks = height // size
    deep = per * rows
    nc = size // deep
    gcuts, scuts = (
        sum((end - first) * cut for first, end, cut in plan) for plan in (gplan, splan))
    gwide, swide = height - (ny - 1) * gcuts, height - (ny - 1) * scuts
    f32 = jnp.float32

    barrier = pltpu.get_barrier_semaphore()

    @pl.when(z > 0)
    def _():
        pl.semaphore_signal(barrier, inc=1, device_id={"fsdp": z - 1}, device_id_type=MESH)

    @pl.when(z < nz - 1)
    def _():
        pl.semaphore_signal(barrier, inc=1, device_id={"fsdp": z + 1}, device_id_type=MESH)

    for i in range(1, nt):
        pl.semaphore_signal(
            barrier, inc=1, device_id={"tensor": lax.rem(t + i, nt)}, device_id_type=MESH)
    for i in range(1, ny):
        pl.semaphore_signal(
            barrier, inc=1, device_id={"dp": lax.rem(y + i, ny)}, device_id_type=MESH)

    in_copies = [
        pltpu.make_async_copy(src, dst, local_sem.at[i])
        for i, (src, dst) in enumerate(
            [(low_in_hbm, lin), (panels_hbm, pan.at[z]), (low_out_hbm, lout), (cot_hbm, cot),
             (rows_hbm, rows_ref)]
        )
    ]
    feature_blocks, toks = tok.shape[:2]

    def token_copy(b):
        return pltpu.make_async_copy(
            tokens_hbm.at[:, pl.ds(pl.multiple_of(b * blk, blk), blk)], tok.at[b], tok_sem.at[b])

    blocks = lin.shape[0] // blk

    def in_turn(b):
        return lax.rem(t * blocks + b, feature_blocks)

    def token_start(b, carry):
        token_copy(in_turn(b)).start()
        return carry

    def token_wait(b, carry):
        token_copy(in_turn(b)).wait()
        return carry

    in_copies[0].start()
    lax.fori_loop(0, feature_blocks, token_start, 0)
    for copy in in_copies[1:]:
        copy.start()

    neighbours = jnp.where(z > 0, 1, 0) + jnp.where(z < nz - 1, 1, 0)
    pl.semaphore_wait(barrier, nt - 1 + ny - 1 + neighbours)

    def reach(j, cut):
        return pl.ds(pl.multiple_of(j * size + y * cut, 8), size - (ny - 1) * cut)

    def alone(j, p, cut):
        first = p * ((size - cut) // max(ny - 1, 1))
        return pl.ds(pl.multiple_of(j * size + first, 8), cut)

    def gather_copy(way, shard, j, cut, from_input=False):
        there = z + 1 if way == 0 else z - 1
        at = reach(j, cut)
        return pltpu.make_async_remote_copy(
            src_ref=panels_hbm.at[at] if from_input else pan.at[shard, at],
            dst_ref=pan.at[shard, at],
            send_sem=ag_send.at[way, shard], recv_sem=ag_recv.at[shard, j],
            device_id={"fsdp": there}, device_id_type=MESH)

    def across_copy(i, shard, j, cut):
        at = alone(j, y, cut)
        return pltpu.make_async_remote_copy(
            src_ref=pan.at[shard, at], dst_ref=pan.at[shard, at],
            send_sem=ay_send.at[shard], recv_sem=ay_recv.at[i, j],
            device_id={"dp": lax.rem(y + i, ny)}, device_id_type=MESH)

    def send_own(way, j):
        @pl.when(j < chunks)
        def _():
            by_cut(gplan, j, lambda cut: gather_copy(way, z, j, cut, True).start())

    def inside(j):
        return jnp.logical_and(j >= 0, j < chunks)

    up_ahead = jnp.where(z == 0, AHEAD_END, AHEAD)
    down_ahead = jnp.where(z == nz - 1, AHEAD_END, AHEAD)

    def first_own(j, carry):
        pl.when(jnp.logical_and(z < nz - 1, j < up_ahead))(lambda: send_own(0, j))
        pl.when(jnp.logical_and(z > 0, j < down_ahead))(lambda: send_own(1, j))
        return carry

    lax.fori_loop(0, max(AHEAD, AHEAD_END), first_own, 0)

    def pass_on(h, tau):
        j = tau - (h - 1) * GATHER_LAG

        def arrived(way, shard, more):
            def act(cut):
                gather_copy(way, shard, j, cut).wait_recv()

                @pl.when(more)
                def _():
                    gather_copy(way, shard, j, cut).start()

                if cut:
                    for i in range(1, ny):
                        across_copy(i, shard, j, cut).start()

            by_cut(gplan, j, act)

        @pl.when(jnp.logical_and(inside(j), z - h >= 0))
        def _():
            arrived(0, z - h, z < nz - 1)

        @pl.when(jnp.logical_and(inside(j), z + h < nz))
        def _():
            arrived(1, z + h, z > 0)

    def across_done(j):
        def act(cut):
            if cut:
                at = pan.at[pl.ds(0, nz - 1), pl.ds(0, cut)]
                for i in range(1, ny):
                    pltpu.make_async_copy(at, at, ay_recv.at[i, j]).wait()

        by_cut(gplan, j, act)

    pairs = nt // 2
    pair, side = t // 2, lax.rem(t, 2)

    def lat_pair():
        return pltpu.make_async_remote_copy(
            src_ref=lpart.at[1 - side], dst_ref=lpair,
            send_sem=l0_send, recv_sem=l0_recv,
            device_id={"tensor": 2 * pair + 1 - side}, device_id_type=MESH)

    def lat_one(i):
        peer = lax.rem(pair + i, pairs)
        return pltpu.make_async_remote_copy(
            src_ref=lhalf.at[peer], dst_ref=lrecv.at[i],
            send_sem=l1_send.at[i], recv_sem=l1_recv.at[i],
            device_id={"tensor": 2 * peer + side}, device_id_type=MESH)

    def lat_two(i, shard):
        peer = lax.rem(t + i, nt)
        return pltpu.make_async_remote_copy(
            src_ref=lat.at[shard], dst_ref=lat.at[shard],
            send_sem=l2_send.at[i], recv_sem=l2_recv.at[i],
            device_id={"tensor": peer}, device_id_type=MESH)

    def latent_part():
        in_copies[0].wait()
        lax.fori_loop(0, blocks, token_wait, 0)
        lpart[...] = jnp.dot(
            jnp.concatenate([tok[t * blocks + b] for b in range(blocks)], axis=1), lin[...],
            preferred_element_type=f32,
        ).reshape(lpart.shape)
        lat_pair().start()

    def latent_half():
        lat_pair().wait_recv()
        lhalf[...] = lpart[side] + lpair[...]
        for i in range(1, pairs):
            lat_one(i).start()

    def latent_sum():
        total = lhalf[pair]
        for i in range(1, pairs):
            lat_one(i).wait_recv()
            total = total + lrecv[i]
        mine = side * pairs + pair
        lat[mine] = total.astype(lat.dtype)
        for i in range(1, nt):
            lat_two(i, mine).start()
        lax.fori_loop(blocks, feature_blocks, token_wait, 0)
        for copy in in_copies[1:]:
            copy.wait()

    def latent_done():
        for i in range(1, nt):
            sender = lax.rem(t + nt - i, nt)
            lat_two(i, lax.rem(sender, 2) * pairs + sender // 2).wait_recv()

    def column(c):
        picked = jnp.concatenate([tok[rows_ref[k, c]] for k in range(per)], axis=1)
        lines = pl.ds(pl.multiple_of(c * deep, 8), deep)
        parts = [pan[s, lines] for s in range(nz)]
        weight = jnp.concatenate(
            [parts[s][k * rows:(k + 1) * rows] for k in range(per) for s in range(nz)], axis=0)
        latent = lat[...].reshape(toks, -1)
        pre = jnp.dot(latent, lout[c], preferred_element_type=f32)
        pre = pre + jnp.dot(picked, weight, preferred_element_type=f32)
        at = pl.ds(pl.multiple_of(c * blk, blk), blk)
        square = pre * pre
        curve = jnp.tanh(GELU_SCALE * (pre + GELU_CUBIC * (square * pre)))
        half = 0.5 * (1.0 + curve)
        act_ref[:, at] = (pre * half).astype(act_ref.dtype)
        inner = GELU_SCALE * (1.0 + 3.0 * GELU_CUBIC * square)
        deriv = half + 0.5 * pre * (1.0 - curve * curve) * inner
        slope = (cot[:, at].astype(f32) * deriv).astype(jnp.bfloat16)
        grad = lax.dot_general(
            picked, slope, (((0,), (0,)), ((), ())), preferred_element_type=f32)
        for d in range(nz):
            own[d, lines] = jnp.concatenate(
                [grad[k * blk + d * rows:k * blk + (d + 1) * rows] for k in range(per)], axis=0)

    def landing(j, cut):
        return pl.ds(pl.multiple_of(j * (size // ny), 8), cut)

    def early_copy(i, j, cut):
        peer = lax.rem(y + i, ny)
        return pltpu.make_async_remote_copy(
            src_ref=xsend.at[:, alone(j, peer, cut)],
            dst_ref=xrecv.at[i - 1, :, landing(j, cut)],
            send_sem=x_send.at[i], recv_sem=x_recv.at[i, j],
            device_id={"dp": peer}, device_id_type=MESH)

    def early_start(j):
        def act(cut):
            if cut:
                for i in range(1, ny):
                    at = alone(j, lax.rem(y + i, ny), cut)
                    xsend[:, at] = own[:, at].astype(xsend.dtype)
                    early_copy(i, j, cut).start()

        by_cut(splan, j, act)

    def early_done(j):
        def act(cut):
            if cut:
                at = alone(j, y, cut)
                total = own[:, at]
                for i in range(1, ny):
                    early_copy(i, j, cut).wait_recv()
                    total = total + xrecv[i - 1, :, landing(j, cut)].astype(f32)
                own[:, at] = total

        by_cut(splan, j, act)

    def sum_copy(way, d, j, cut):
        there = z + 1 if way == 0 else z - 1
        at = reach(j, cut)
        return pltpu.make_async_remote_copy(
            src_ref=sbuf.at[d, at], dst_ref=rbuf.at[way, d, at],
            send_sem=rs_send.at[d], recv_sem=rs_recv.at[way, d, j],
            device_id={"fsdp": there}, device_id_type=MESH)

    def flow(way, d, j, first):
        def act(cut):
            at = reach(j, cut)

            @pl.when(first)
            def _():
                sbuf[d, at] = own[d, at].astype(sbuf.dtype)

            @pl.when(jnp.logical_not(first))
            def _():
                sum_copy(way, d, j, cut).wait_recv()
                sbuf[d, at] = (own[d, at] + rbuf[way, d, at].astype(f32)).astype(sbuf.dtype)

            sum_copy(way, d, j, cut).start()

        by_cut(splan, j, act)

    def final_copy(i, j, cut):
        at = reach(j, cut)
        return pltpu.make_async_remote_copy(
            src_ref=ysend.at[at], dst_ref=yrecv.at[i - 1, at],
            send_sem=y_send.at[i], recv_sem=y_recv.at[i, j],
            device_id={"dp": lax.rem(y + i, ny)}, device_id_type=MESH)

    def finish(j):
        def act(cut):
            at = reach(j, cut)

            def landed(way):
                sum_copy(way, z, j, cut).wait_recv()
                return rbuf[way, z, at].astype(f32)

            @pl.when(z == 0)
            def _():
                ysend[at] = (own[z, at] + landed(1)).astype(ysend.dtype)

            @pl.when(z == nz - 1)
            def _():
                ysend[at] = (own[z, at] + landed(0)).astype(ysend.dtype)

            @pl.when(jnp.logical_and(z > 0, z < nz - 1))
            def _():
                ysend[at] = (own[z, at] + landed(0) + landed(1)).astype(ysend.dtype)

            for i in range(1, ny):
                final_copy(i, j, cut).start()

        by_cut(splan, j, act)

    def result(j):
        def act(cut):
            for i in range(1, ny):
                peer = lax.rem(y + ny - i, ny)
                at = pl.ds(pl.multiple_of(j * size + peer * cut, 8), size - (ny - 1) * cut)
                pltpu.make_async_copy(
                    yrecv.at[i - 1, at], yrecv.at[i - 1, at], y_recv.at[i, j]).wait()
            if cut:
                mine = alone(j, y, cut)
                grad_ref[mine] = ysend[mine].astype(f32)
                for i in range(1, ny):
                    there = alone(j, lax.rem(y + ny - i, ny), cut)
                    grad_ref[there] = yrecv[i - 1, there].astype(f32)
            if size - ny * cut:
                shared = pl.ds(pl.multiple_of(j * size + (ny - 1) * cut, 8), size - ny * cut)
                value = ysend[shared].astype(f32)
                for i in range(1, ny):
                    value = value + yrecv[i - 1, shared].astype(f32)
                grad_ref[shared] = value

        by_cut(splan, j, act)

    compute_at = (nz - 2) * GATHER_LAG + ACROSS_LAG
    sum_at = compute_at + EARLY_LAG
    finish_at = sum_at + (nz - 1) * SUM_LAG
    steps = chunks + finish_at + FINAL_LAG

    def gathers(tau):
        def hop(k, carry):
            pass_on(nz - 1 - k, tau)
            return carry

        lax.fori_loop(0, nz - 1, hop, 0)
        pl.when(z < nz - 1)(lambda: send_own(0, tau + up_ahead))
        pl.when(z > 0)(lambda: send_own(1, tau + down_ahead))

    def sums(tau):
        summed = tau - sum_at
        pl.when(inside(summed))(lambda: early_done(summed))
        up, down = summed - z * SUM_LAG, summed - (nz - 1 - z) * SUM_LAG

        def towards(d, carry):
            far = nz - 1 - d

            @pl.when(jnp.logical_and(far > z, inside(up)))
            def _():
                flow(0, far, up, z == 0)

            @pl.when(jnp.logical_and(d < z, inside(down)))
            def _():
                flow(1, d, down, z == nz - 1)

            return carry

        lax.fori_loop(0, nz, towards, 0)
        last = tau - finish_at
        pl.when(inside(last))(lambda: finish(last))
        done = last - FINAL_LAG
        pl.when(inside(done))(lambda: result(done))

    def latents(tau):
        pl.when(tau == 0)(latent_half)
        pl.when(tau == 1)(latent_sum)
        pl.when(tau == compute_at)(latent_done)

    def columns(tau):
        now = tau - compute_at

        @pl.when(inside(now))
        def _():
            across_done(now)
            for i in range(nc):
                column(now * nc + i)
            early_start(now)

    stages = {"g": gathers, "s": sums, "l": latents, "r": columns}

    def step(tau, carry):
        for name in ORDER:
            stages[name](tau)
        return carry

    latent_part()
    lax.fori_loop(0, steps, step, 0)

    lat_pair().wait_send()
    for i in range(1, pairs):
        lat_one(i).wait_send()
    for i in range(1, nt):
        lat_two(i, side * pairs + pair).wait_send()

    def gather_left(way, s):
        at = pan.at[s, pl.ds(0, gwide)]
        pltpu.make_async_copy(at, at, ag_send.at[way, s]).wait()

    def left(s, carry):
        @pl.when(jnp.logical_and(s <= z, z < nz - 1))
        def _():
            gather_left(0, s)

        @pl.when(jnp.logical_and(s >= z, z > 0))
        def _():
            gather_left(1, s)

        @pl.when(s != z)
        def _():
            if gcuts:
                at = pan.at[s, pl.ds(0, gcuts)]
                for i in range(1, ny):
                    pltpu.make_async_copy(at, at, ay_send.at[s]).wait()
            at = sbuf.at[s, pl.ds(0, swide)]
            pltpu.make_async_copy(at, at, rs_send.at[s]).wait()

        return carry

    lax.fori_loop(0, nz, left, 0)
    for i in range(1, ny):
        at = ysend.at[pl.ds(0, swide)]
        pltpu.make_async_copy(at, at, y_send.at[i]).wait()
        if scuts:
            at = xsend.at[:, pl.ds(0, scuts)]
            pltpu.make_async_copy(at, at, x_send.at[i]).wait()


def write_out(act_in, grad_in, act_out, grad_out, sem):
    copies = []
    for a, (src, dst) in enumerate([(act_in, act_out), (grad_in, grad_out)]):
        step = src.shape[0] // PIECES
        for i in range(PIECES):
            at = pl.ds(i * step, step)
            copies.append(pltpu.make_async_copy(src.at[at], dst.at[at], sem.at[a, i]))
    for copy in copies:
        copy.start()
    for copy in copies:
        copy.wait()


def on_device(sizes, tokens, panels, block_rows, low_in, low_out, cotangent):
    nz, ny, nt = sizes
    cols, per, rows, blk = panels.shape
    toks, rank = tokens.shape[0], low_in.shape[1]
    nc = COLS if ny <= 2 and cols % COLS == 0 else 4 if cols % 4 == 0 else 1
    chunks = cols // nc
    size = nc * per * rows

    def plan_of(cuts):
        if ny != 2:
            return ((0, chunks, 0 if ny == 1 else size // ny),)
        plan, first = [], 0
        for end, cut in cuts:
            end = end * chunks // 14
            if end > first:
                plan.append((first, end, size * cut // 16 // 16 * 16))
            first = max(first, end)
        return tuple(plan)

    bf16, f32 = jnp.bfloat16, jnp.float32
    hop_type = bf16 if nz <= 4 and ny <= 2 else f32
    low_out = low_out.reshape(cols, rank, blk)
    lines = panels.reshape(cols * per * rows, blk)
    height = lines.shape[0]
    hbm = pl.BlockSpec(memory_space=pl.ANY)
    vmem = pl.BlockSpec(memory_space=pltpu.VMEM)
    dma = pltpu.SemaphoreType.DMA
    others = max(ny - 1, 1)
    activated, grad = pl.pallas_call(
        functools.partial(
            kernel, nz, ny, nt, per, rows, size, plan_of(GATHER_CUT), plan_of(SUM_CUT)),
        out_shape=(
            pltpu.VMEM(cotangent.shape, bf16),
            pltpu.VMEM(lines.shape, f32),
        ),
        in_specs=[hbm] * 6,
        out_specs=(vmem, vmem),
        scratch_shapes=[
            pltpu.SMEM((per, cols), jnp.int32),
            pltpu.VMEM((tokens.shape[1] // blk, toks, blk), bf16),
            pltpu.VMEM(low_in.shape, bf16),
            pltpu.VMEM(low_out.shape, bf16),
            pltpu.VMEM(cotangent.shape, bf16),
            pltpu.VMEM((nz, height, blk), bf16),
            pltpu.VMEM((nz, height, blk), f32),
            pltpu.VMEM((nz, height, blk), hop_type),
            pltpu.VMEM((2, nz, height, blk), hop_type),
            pltpu.VMEM((height, blk), hop_type),
            pltpu.VMEM((others, height, blk), hop_type),
            pltpu.VMEM((nz, height, blk), hop_type),
            pltpu.VMEM((others, nz, height // ny, blk), hop_type),
            pltpu.VMEM((2, nt // 2, toks // nt, rank), f32),
            pltpu.VMEM((nt // 2, toks // nt, rank), f32),
            pltpu.VMEM((nt // 2, toks // nt, rank), f32),
            pltpu.VMEM((nt // 2, toks // nt, rank), f32),
            pltpu.VMEM((nt, toks // nt, rank), bf16),
            dma((5,)),
            dma((tokens.shape[1] // blk,)),
            dma((2, nz)),
            dma((nz, chunks)),
            dma((nz,)),
            dma((ny, chunks)),
            dma((nz,)),
            dma((2, nz, chunks)),
            dma((ny,)),
            dma((ny, chunks)),
            dma((ny,)),
            dma((ny, chunks)),
            dma,
            dma,
            dma((nt,)),
            dma((nt,)),
            dma((nt,)),
            dma((nt,)),
        ],
        compiler_params=pltpu.CompilerParams(
            collective_id=0, has_side_effects=True, vmem_limit_bytes=52 * 1024 * 1024),
    )(tokens, lines, block_rows.T, low_in, low_out, cotangent)
    activated, grad = pl.pallas_call(
        write_out,
        out_shape=(
            jax.ShapeDtypeStruct(cotangent.shape, bf16),
            jax.ShapeDtypeStruct(lines.shape, f32),
        ),
        in_specs=[vmem, vmem],
        out_specs=(hbm, hbm),
        scratch_shapes=[dma((2, PIECES))],
        compiler_params=pltpu.CompilerParams(vmem_limit_bytes=1024 * 1024),
    )(pltpu.with_memory_space_constraint(activated, pltpu.VMEM), pltpu.with_memory_space_constraint(grad, pltpu.VMEM))
    return activated, grad.reshape(panels.shape)


def solution(mesh):
    in_specs = (
        P(("fsdp", "dp"), None),
        P("tensor", None, "fsdp", None),
        P("tensor", None),
        P("tensor", None),
        P("tensor", None, None, None),
        P(("fsdp", "dp"), "tensor"),
    )
    out_specs = (P(("fsdp", "dp"), "tensor"), P("tensor", None, "fsdp", None))
    sizes = tuple(mesh.shape[name] for name in ("fsdp", "dp", "tensor"))
    return jax.shard_map(
        functools.partial(on_device, sizes),
        mesh=mesh, in_specs=in_specs, out_specs=out_specs, check_vma=False,
    )
```

```python
import functools
import math

import jax
import jax.numpy as jnp
from jax import lax
from jax.experimental import pallas as pl
from jax.experimental.pallas import tpu as pltpu
from jax.sharding import PartitionSpec as P

MESH = pl.DeviceIdType.MESH
GELU_SCALE = math.sqrt(2.0 / math.pi)
GELU_CUBIC = 0.044715
COLS = 2
AHEAD = 4
AHEAD_END = 14
GATHER_LAG = 2
ACROSS_LAG = 1
EARLY_LAG = 2
SUM_LAG = 4
FINAL_LAG = 4
GATHER_CUT = ((5, 8), (12, 5), (14, 0))
SUM_CUT = ((4, 3), (10, 5), (14, 7))
PIECES = 1
GATHER_WARP = 1
SUM_WARP = 6
ORDER = "glrs"


def by_cut(plan, j, act):
    if len(plan) == 1:
        act(plan[0][2])
    else:
        for first, end, cut in plan:
            pl.when(jnp.logical_and(j >= first, j < end))(functools.partial(act, cut))


def kernel(
    nz, ny, nt, per, rows, size, gplan, splan,
    tokens_hbm, panels_hbm, rows_hbm, low_in_hbm, low_out_hbm, cot_hbm,
    act_ref, grad_ref,
    rows_ref, tok, lin, lout, cot, pan, own, sbuf, rbuf, ysend, yrecv, xsend, xrecv,
    lpart, lpair, lhalf, lrecv, lat,
    local_sem, tok_sem, ag_send, ag_recv, ay_send, ay_recv, rs_send, rs_recv,
    y_send, y_recv, x_send, x_recv, l0_send, l0_recv, l1_send, l1_recv, l2_send, l2_recv,
):
    z, y, t = lax.axis_index("fsdp"), lax.axis_index("dp"), lax.axis_index("tensor")
    height, blk = panels_hbm.shape
    chunks = height // size
    deep = per * rows
    nc = size // deep
    gcuts, scuts = (
        sum((end - first) * cut for first, end, cut in plan) for plan in (gplan, splan))
    gwide, swide = height - (ny - 1) * gcuts, height - (ny - 1) * scuts
    f32 = jnp.float32

    barrier = pltpu.get_barrier_semaphore()

    @pl.when(z > 0)
    def _():
        pl.semaphore_signal(barrier, inc=1, device_id={"fsdp": z - 1}, device_id_type=MESH)

    @pl.when(z < nz - 1)
    def _():
        pl.semaphore_signal(barrier, inc=1, device_id={"fsdp": z + 1}, device_id_type=MESH)

    for i in range(1, nt):
        pl.semaphore_signal(
            barrier, inc=1, device_id={"tensor": lax.rem(t + i, nt)}, device_id_type=MESH)
    for i in range(1, ny):
        pl.semaphore_signal(
            barrier, inc=1, device_id={"dp": lax.rem(y + i, ny)}, device_id_type=MESH)

    in_copies = [
        pltpu.make_async_copy(src, dst, local_sem.at[i])
        for i, (src, dst) in enumerate(
            [(low_in_hbm, lin), (panels_hbm, pan.at[z]), (low_out_hbm, lout), (cot_hbm, cot),
             (rows_hbm, rows_ref)]
        )
    ]
    feature_blocks, toks = tok.shape[:2]

    def token_copy(b):
        return pltpu.make_async_copy(
            tokens_hbm.at[:, pl.ds(pl.multiple_of(b * blk, blk), blk)], tok.at[b], tok_sem.at[b])

    blocks = lin.shape[0] // blk

    def in_turn(b):
        return lax.rem(t * blocks + b, feature_blocks)

    def token_start(b, carry):
        token_copy(in_turn(b)).start()
        return carry

    def token_wait(b, carry):
        token_copy(in_turn(b)).wait()
        return carry

    in_copies[0].start()
    lax.fori_loop(0, blocks, token_start, 0)

    neighbours = jnp.where(z > 0, 1, 0) + jnp.where(z < nz - 1, 1, 0)
    pl.semaphore_wait(barrier, nt - 1 + ny - 1 + neighbours)

    pairs = nt // 2
    pair, side = t // 2, lax.rem(t, 2)

    def lat_pair():
        return pltpu.make_async_remote_copy(
            src_ref=lpart.at[1 - side], dst_ref=lpair,
            send_sem=l0_send, recv_sem=l0_recv,
            device_id={"tensor": 2 * pair + 1 - side}, device_id_type=MESH)

    def lat_one(i):
        peer = lax.rem(pair + i, pairs)
        return pltpu.make_async_remote_copy(
            src_ref=lhalf, dst_ref=lrecv.at[i],
            send_sem=l1_send.at[i], recv_sem=l1_recv.at[i],
            device_id={"tensor": 2 * peer + side}, device_id_type=MESH)

    def lat_two(half):
        return pltpu.make_async_remote_copy(
            src_ref=lat.at[half], dst_ref=lat.at[half],
            send_sem=l2_send, recv_sem=l2_recv,
            device_id={"tensor": 2 * pair + 1 - side}, device_id_type=MESH)

    def latent_half():
        lat_pair().wait_recv()
        half = lpart[side] + lpair[...]
        lpart[side] = half
        lhalf[...] = half.astype(lhalf.dtype)
        for i in range(1, pairs):
            lat_one(i).start()

    def latent_sum():
        total = lpart[side]
        for i in range(1, pairs):
            lat_one(i).wait_recv()
            total = total + lrecv[i].astype(f32)
        lat[side] = total.astype(lat.dtype)
        lat_two(side).start()
        lax.fori_loop(blocks, feature_blocks, token_wait, 0)
        for copy in in_copies[1:]:
            copy.wait()

    def latent_done():
        lat_two(1 - side).wait_recv()

    def reach(j, cut):
        return pl.ds(pl.multiple_of(j * size + y * cut, 8), size - (ny - 1) * cut)

    def alone(j, p, cut):
        first = p * ((size - cut) // max(ny - 1, 1))
        return pl.ds(pl.multiple_of(j * size + first, 8), cut)

    def gather_copy(way, shard, j, cut, from_input=False):
        there = z + 1 if way == 0 else z - 1
        at = reach(j, cut)
        return pltpu.make_async_remote_copy(
            src_ref=panels_hbm.at[at] if from_input else pan.at[shard, at],
            dst_ref=pan.at[shard, at],
            send_sem=ag_send.at[way, shard], recv_sem=ag_recv.at[shard, j],
            device_id={"fsdp": there}, device_id_type=MESH)

    def across_copy(i, shard, j, cut):
        at = alone(j, y, cut)
        return pltpu.make_async_remote_copy(
            src_ref=pan.at[shard, at], dst_ref=pan.at[shard, at],
            send_sem=ay_send.at[shard], recv_sem=ay_recv.at[i, j],
            device_id={"dp": lax.rem(y + i, ny)}, device_id_type=MESH)

    def send_own(way, j):
        @pl.when(j < chunks)
        def _():
            by_cut(gplan, j, lambda cut: gather_copy(way, z, j, cut, True).start())

    def inside(j):
        return jnp.logical_and(j >= 0, j < chunks)

    up_ahead = jnp.where(z == 0, AHEAD_END, AHEAD)
    down_ahead = jnp.where(z == nz - 1, AHEAD_END, AHEAD)

    def first_own(j, carry):
        pl.when(jnp.logical_and(z < nz - 1, j < up_ahead))(lambda: send_own(0, j))
        pl.when(jnp.logical_and(z > 0, j < down_ahead))(lambda: send_own(1, j))
        return carry

    lax.fori_loop(0, max(AHEAD, AHEAD_END), first_own, 0)

    in_copies[0].wait()
    lax.fori_loop(0, blocks, token_wait, 0)
    lpart[...] = jnp.dot(
        jnp.concatenate([tok[t * blocks + b] for b in range(blocks)], axis=1), lin[...],
        preferred_element_type=f32,
    ).reshape(lpart.shape)

    lat_pair().start()
    lax.fori_loop(blocks, feature_blocks, token_start, 0)
    for copy in in_copies[1:]:
        copy.start()

    def front(h, tau):
        grown = lax.max(tau - GATHER_WARP - (h - 1), 0)
        return tau - (h - 1) + lax.min(grown, (nz - 1 - h) * (GATHER_LAG - 1))

    def pass_on(h, j):
        def arrived(way, shard, more):
            def act(cut):
                gather_copy(way, shard, j, cut).wait_recv()

                @pl.when(more)
                def _():
                    gather_copy(way, shard, j, cut).start()

                if cut:
                    for i in range(1, ny):
                        across_copy(i, shard, j, cut).start()

            by_cut(gplan, j, act)

        @pl.when(jnp.logical_and(inside(j), z - h >= 0))
        def _():
            arrived(0, z - h, z < nz - 1)

        @pl.when(jnp.logical_and(inside(j), z + h < nz))
        def _():
            arrived(1, z + h, z > 0)

    def across_done(j):
        def act(cut):
            if cut:
                at = pan.at[pl.ds(0, nz - 1), pl.ds(0, cut)]
                for i in range(1, ny):
                    pltpu.make_async_copy(at, at, ay_recv.at[i, j]).wait()

        by_cut(gplan, j, act)

    def column(c):
        picked = jnp.concatenate([tok[rows_ref[k, c]] for k in range(per)], axis=1)
        lines = pl.ds(pl.multiple_of(c * deep, 8), deep)
        parts = [pan[s, lines] for s in range(nz)]
        weight = jnp.concatenate(
            [parts[s][k * rows:(k + 1) * rows] for k in range(per) for s in range(nz)], axis=0)
        latent = lat[...].reshape(toks, -1)
        pre = jnp.dot(latent, lout[c], preferred_element_type=f32)
        pre = pre + jnp.dot(picked, weight, preferred_element_type=f32)
        at = pl.ds(pl.multiple_of(c * blk, blk), blk)
        square = pre * pre
        curve = jnp.tanh(GELU_SCALE * (pre + GELU_CUBIC * (square * pre)))
        half = 0.5 * (1.0 + curve)
        act_ref[:, at] = (pre * half).astype(act_ref.dtype)
        inner = GELU_SCALE * (1.0 + 3.0 * GELU_CUBIC * square)
        deriv = half + 0.5 * pre * (1.0 - curve * curve) * inner
        slope = (cot[:, at].astype(f32) * deriv).astype(jnp.bfloat16)
        grad = lax.dot_general(
            picked, slope, (((0,), (0,)), ((), ())), preferred_element_type=f32)
        for d in range(nz):
            own[d, lines] = jnp.concatenate(
                [grad[k * blk + d * rows:k * blk + (d + 1) * rows] for k in range(per)], axis=0)

    def landing(j, cut):
        return pl.ds(pl.multiple_of(j * (size // ny), 8), cut)

    def early_copy(i, j, cut):
        peer = lax.rem(y + i, ny)
        return pltpu.make_async_remote_copy(
            src_ref=xsend.at[:, alone(j, peer, cut)],
            dst_ref=xrecv.at[i - 1, :, landing(j, cut)],
            send_sem=x_send.at[i], recv_sem=x_recv.at[i, j],
            device_id={"dp": peer}, device_id_type=MESH)

    def early_start(j):
        def act(cut):
            if cut:
                for i in range(1, ny):
                    at = alone(j, lax.rem(y + i, ny), cut)
                    xsend[:, at] = own[:, at].astype(xsend.dtype)
                    early_copy(i, j, cut).start()

        by_cut(splan, j, act)

    def early_done(j):
        def act(cut):
            if cut:
                at = alone(j, y, cut)
                total = own[:, at]
                for i in range(1, ny):
                    early_copy(i, j, cut).wait_recv()
                    total = total + xrecv[i - 1, :, landing(j, cut)].astype(f32)
                own[:, at] = total

        by_cut(splan, j, act)

    def sum_copy(way, d, j, cut):
        there = z + 1 if way == 0 else z - 1
        at = reach(j, cut)
        return pltpu.make_async_remote_copy(
            src_ref=sbuf.at[d, at], dst_ref=rbuf.at[way, d, at],
            send_sem=rs_send.at[d], recv_sem=rs_recv.at[way, d, j],
            device_id={"fsdp": there}, device_id_type=MESH)

    def flow(way, d, j, first):
        def act(cut):
            at = reach(j, cut)

            @pl.when(first)
            def _():
                sbuf[d, at] = own[d, at].astype(sbuf.dtype)

            @pl.when(jnp.logical_not(first))
            def _():
                sum_copy(way, d, j, cut).wait_recv()
                sbuf[d, at] = (own[d, at] + rbuf[way, d, at].astype(f32)).astype(sbuf.dtype)

            sum_copy(way, d, j, cut).start()

        by_cut(splan, j, act)

    def final_copy(i, j, cut):
        at = reach(j, cut)
        return pltpu.make_async_remote_copy(
            src_ref=ysend.at[at], dst_ref=yrecv.at[i - 1, at],
            send_sem=y_send.at[i], recv_sem=y_recv.at[i, j],
            device_id={"dp": lax.rem(y + i, ny)}, device_id_type=MESH)

    def finish(j):
        def act(cut):
            at = reach(j, cut)

            def landed(way):
                sum_copy(way, z, j, cut).wait_recv()
                return rbuf[way, z, at].astype(f32)

            @pl.when(z == 0)
            def _():
                ysend[at] = (own[z, at] + landed(1)).astype(ysend.dtype)

            @pl.when(z == nz - 1)
            def _():
                ysend[at] = (own[z, at] + landed(0)).astype(ysend.dtype)

            @pl.when(jnp.logical_and(z > 0, z < nz - 1))
            def _():
                ysend[at] = (own[z, at] + landed(0) + landed(1)).astype(ysend.dtype)

            for i in range(1, ny):
                final_copy(i, j, cut).start()

        by_cut(splan, j, act)

    def result(j):
        def act(cut):
            for i in range(1, ny):
                peer = lax.rem(y + ny - i, ny)
                at = pl.ds(pl.multiple_of(j * size + peer * cut, 8), size - (ny - 1) * cut)
                pltpu.make_async_copy(
                    yrecv.at[i - 1, at], yrecv.at[i - 1, at], y_recv.at[i, j]).wait()
            if cut:
                mine = alone(j, y, cut)
                grad_ref[mine] = ysend[mine].astype(f32)
                for i in range(1, ny):
                    there = alone(j, lax.rem(y + ny - i, ny), cut)
                    grad_ref[there] = yrecv[i - 1, there].astype(f32)
            if size - ny * cut:
                shared = pl.ds(pl.multiple_of(j * size + (ny - 1) * cut, 8), size - ny * cut)
                value = ysend[shared].astype(f32)
                for i in range(1, ny):
                    value = value + yrecv[i - 1, shared].astype(f32)
                grad_ref[shared] = value

        by_cut(splan, j, act)

    compute_at = nz - 2 + ACROSS_LAG
    sum_at = compute_at + EARLY_LAG
    finish_at = sum_at + (nz - 1) * SUM_LAG
    steps = chunks + finish_at + FINAL_LAG

    def gathers(tau):
        def hop(k, carry):
            h = nz - 1 - k

            def each(j, carry):
                pass_on(h, j)
                return carry

            lax.fori_loop(front(h, tau), front(h, tau + 1), each, 0)
            return carry

        lax.fori_loop(0, nz - 1, hop, 0)

        def own_next(j, carry):
            pl.when(z < nz - 1)(lambda: send_own(0, j + up_ahead))
            pl.when(z > 0)(lambda: send_own(1, j + down_ahead))
            return carry

        lax.fori_loop(front(1, tau), front(1, tau + 1), own_next, 0)

    def early_front(tau):
        return tau - compute_at - 1 - lax.min(lax.max(tau - SUM_WARP, 0), EARLY_LAG - 1)

    def sums(tau):
        moved = early_front(tau) > early_front(tau - 1)
        fresh = jnp.where(moved, early_front(tau), -1)
        pl.when(inside(fresh))(lambda: early_done(fresh))
        summed = tau - sum_at
        up = jnp.where(z == 0, fresh, summed - z * SUM_LAG)
        down = jnp.where(z == nz - 1, fresh, summed - (nz - 1 - z) * SUM_LAG)

        def towards(d, carry):
            far = nz - 1 - d

            @pl.when(jnp.logical_and(far > z, inside(up)))
            def _():
                flow(0, far, up, z == 0)

            @pl.when(jnp.logical_and(d < z, inside(down)))
            def _():
                flow(1, d, down, z == nz - 1)

            return carry

        lax.fori_loop(0, nz, towards, 0)
        last = tau - finish_at
        pl.when(inside(last))(lambda: finish(last))
        done = last - FINAL_LAG
        pl.when(inside(done))(lambda: result(done))

    def latents(tau):
        pl.when(tau == 0)(latent_half)
        pl.when(tau == 1)(latent_sum)
        pl.when(tau == compute_at)(latent_done)

    def columns(tau):
        now = tau - compute_at

        @pl.when(inside(now))
        def _():
            across_done(now)
            for i in range(nc):
                column(now * nc + i)
            early_start(now)

    stages = {"g": gathers, "s": sums, "l": latents, "r": columns}

    def step(tau, carry):
        for name in ORDER:
            stages[name](tau)
        return carry

    lax.fori_loop(0, steps, step, 0)

    lat_pair().wait_send()
    for i in range(1, pairs):
        lat_one(i).wait_send()
    lat_two(side).wait_send()

    def gather_left(way, s):
        at = pan.at[s, pl.ds(0, gwide)]
        pltpu.make_async_copy(at, at, ag_send.at[way, s]).wait()

    def left(s, carry):
        @pl.when(jnp.logical_and(s <= z, z < nz - 1))
        def _():
            gather_left(0, s)

        @pl.when(jnp.logical_and(s >= z, z > 0))
        def _():
            gather_left(1, s)

        @pl.when(s != z)
        def _():
            if gcuts:
                at = pan.at[s, pl.ds(0, gcuts)]
                for i in range(1, ny):
                    pltpu.make_async_copy(at, at, ay_send.at[s]).wait()
            at = sbuf.at[s, pl.ds(0, swide)]
            pltpu.make_async_copy(at, at, rs_send.at[s]).wait()

        return carry

    lax.fori_loop(0, nz, left, 0)
    for i in range(1, ny):
        at = ysend.at[pl.ds(0, swide)]
        pltpu.make_async_copy(at, at, y_send.at[i]).wait()
        if scuts:
            at = xsend.at[:, pl.ds(0, scuts)]
            pltpu.make_async_copy(at, at, x_send.at[i]).wait()


def write_out(act_in, grad_in, act_out, grad_out, sem):
    copies = []
    for a, (src, dst) in enumerate([(act_in, act_out), (grad_in, grad_out)]):
        step = src.shape[0] // PIECES
        for i in range(PIECES):
            at = pl.ds(i * step, step)
            copies.append(pltpu.make_async_copy(src.at[at], dst.at[at], sem.at[a, i]))
    for copy in copies:
        copy.start()
    for copy in copies:
        copy.wait()


def on_device(sizes, tokens, panels, block_rows, low_in, low_out, cotangent):
    nz, ny, nt = sizes
    cols, per, rows, blk = panels.shape
    toks, rank = tokens.shape[0], low_in.shape[1]
    nc = COLS if ny <= 2 and cols % COLS == 0 else 4 if cols % 4 == 0 else 1
    chunks = cols // nc
    size = nc * per * rows

    def plan_of(cuts):
        if ny != 2:
            return ((0, chunks, 0 if ny == 1 else size // ny),)
        plan, first = [], 0
        for end, cut in cuts:
            end = end * chunks // 14
            if end > first:
                plan.append((first, end, size * cut // 16 // 16 * 16))
            first = max(first, end)
        return tuple(plan)

    bf16, f32 = jnp.bfloat16, jnp.float32
    hop_type = bf16 if nz <= 4 and ny <= 2 else f32
    low_out = low_out.reshape(cols, rank, blk)
    lines = panels.reshape(cols * per * rows, blk)
    height = lines.shape[0]
    hbm = pl.BlockSpec(memory_space=pl.ANY)
    vmem = pl.BlockSpec(memory_space=pltpu.VMEM)
    dma = pltpu.SemaphoreType.DMA
    others = max(ny - 1, 1)
    activated, grad = pl.pallas_call(
        functools.partial(
            kernel, nz, ny, nt, per, rows, size, plan_of(GATHER_CUT), plan_of(SUM_CUT)),
        out_shape=(
            pltpu.VMEM(cotangent.shape, bf16),
            pltpu.VMEM(lines.shape, f32),
        ),
        in_specs=[hbm] * 6,
        out_specs=(vmem, vmem),
        scratch_shapes=[
            pltpu.SMEM((per, cols), jnp.int32),
            pltpu.VMEM((tokens.shape[1] // blk, toks, blk), bf16),
            pltpu.VMEM(low_in.shape, bf16),
            pltpu.VMEM(low_out.shape, bf16),
            pltpu.VMEM(cotangent.shape, bf16),
            pltpu.VMEM((nz, height, blk), bf16),
            pltpu.VMEM((nz, height, blk), f32),
            pltpu.VMEM((nz, height, blk), hop_type),
            pltpu.VMEM((2, nz, height, blk), hop_type),
            pltpu.VMEM((height, blk), hop_type),
            pltpu.VMEM((others, height, blk), hop_type),
            pltpu.VMEM((nz, height, blk), hop_type),
            pltpu.VMEM((others, nz, height // ny, blk), hop_type),
            pltpu.VMEM((2, toks // 2, rank), f32),
            pltpu.VMEM((toks // 2, rank), f32),
            pltpu.VMEM((toks // 2, rank), f32),
            pltpu.VMEM((nt // 2, toks // 2, rank), f32),
            pltpu.VMEM((2, toks // 2, rank), bf16),
            dma((5,)),
            dma((tokens.shape[1] // blk,)),
            dma((2, nz)),
            dma((nz, chunks)),
            dma((nz,)),
            dma((ny, chunks)),
            dma((nz,)),
            dma((2, nz, chunks)),
            dma((ny,)),
            dma((ny, chunks)),
            dma((ny,)),
            dma((ny, chunks)),
            dma,
            dma,
            dma((nt,)),
            dma((nt,)),
            dma,
            dma,
        ],
        compiler_params=pltpu.CompilerParams(
            collective_id=0, has_side_effects=True, vmem_limit_bytes=52 * 1024 * 1024),
    )(tokens, lines, block_rows.T, low_in, low_out, cotangent)
    activated, grad = pl.pallas_call(
        write_out,
        out_shape=(
            jax.ShapeDtypeStruct(cotangent.shape, bf16),
            jax.ShapeDtypeStruct(lines.shape, f32),
        ),
        in_specs=[vmem, vmem],
        out_specs=(hbm, hbm),
        scratch_shapes=[dma((2, PIECES))],
        compiler_params=pltpu.CompilerParams(vmem_limit_bytes=1024 * 1024),
    )(pltpu.with_memory_space_constraint(activated, pltpu.VMEM), pltpu.with_memory_space_constraint(grad, pltpu.VMEM))
    return activated, grad.reshape(panels.shape)


def solution(mesh):
    in_specs = (
        P(("fsdp", "dp"), None),
        P("tensor", None, "fsdp", None),
        P("tensor", None),
        P("tensor", None),
        P("tensor", None, None, None),
        P(("fsdp", "dp"), "tensor"),
    )
    out_specs = (P(("fsdp", "dp"), "tensor"), P("tensor", None, "fsdp", None))
    sizes = tuple(mesh.shape[name] for name in ("fsdp", "dp", "tensor"))
    return jax.shard_map(
        functools.partial(on_device, sizes),
        mesh=mesh, in_specs=in_specs, out_specs=out_specs, check_vma=False,
    )
```

```python
import functools
import math

import jax
import jax.numpy as jnp
from jax import lax
from jax.experimental import pallas as pl
from jax.experimental.pallas import tpu as pltpu
from jax.sharding import PartitionSpec as P

MESH = pl.DeviceIdType.MESH
GELU_SCALE = math.sqrt(2.0 / math.pi)
GELU_CUBIC = 0.044715
COLS = 2
AHEAD = 4
AHEAD_END = 14
GATHER_LAG = 2
ACROSS_LAG = 1
EARLY_LAG = 2
SUM_LAG = 4
FINAL_LAG = 4
GATHER_CUT = ((5, 8), (12, 5), (14, 0))
SUM_CUT = ((3, 1), (10, 5), (14, 7))
PIECES = 1
GATHER_WARP = 0
SUM_WARP = 6
ORDER = "glrs"


def by_cut(plan, j, act):
    if len(plan) == 1:
        act(plan[0][2])
    else:
        for first, end, cut in plan:
            pl.when(jnp.logical_and(j >= first, j < end))(functools.partial(act, cut))


def kernel(
    nz, ny, nt, per, rows, size, gplan, splan,
    tokens_hbm, panels_hbm, rows_hbm, low_in_hbm, low_out_hbm, cot_hbm,
    act_ref, grad_ref,
    rows_ref, tok, lin, lout, cot, pan, own, sbuf, rbuf, ysend, yrecv, xsend, xrecv,
    lpart, lpair, lhalf, lrecv, lat,
    local_sem, tok_sem, ag_send, ag_recv, ay_send, ay_recv, rs_send, rs_recv,
    y_send, y_recv, x_send, x_recv, l0_send, l0_recv, l1_send, l1_recv, l2_send, l2_recv,
):
    z, y, t = lax.axis_index("fsdp"), lax.axis_index("dp"), lax.axis_index("tensor")
    height, blk = panels_hbm.shape
    chunks = height // size
    deep = per * rows
    nc = size // deep
    gcuts, scuts = (
        sum((end - first) * cut for first, end, cut in plan) for plan in (gplan, splan))
    gwide, swide = height - (ny - 1) * gcuts, height - (ny - 1) * scuts
    f32 = jnp.float32

    barrier = pltpu.get_barrier_semaphore()

    @pl.when(z > 0)
    def _():
        pl.semaphore_signal(barrier, inc=1, device_id={"fsdp": z - 1}, device_id_type=MESH)

    @pl.when(z < nz - 1)
    def _():
        pl.semaphore_signal(barrier, inc=1, device_id={"fsdp": z + 1}, device_id_type=MESH)

    for i in range(1, nt):
        pl.semaphore_signal(
            barrier, inc=1, device_id={"tensor": lax.rem(t + i, nt)}, device_id_type=MESH)
    for i in range(1, ny):
        pl.semaphore_signal(
            barrier, inc=1, device_id={"dp": lax.rem(y + i, ny)}, device_id_type=MESH)

    in_copies = [
        pltpu.make_async_copy(src, dst, local_sem.at[i])
        for i, (src, dst) in enumerate(
            [(low_in_hbm, lin), (panels_hbm, pan.at[z]), (low_out_hbm, lout), (cot_hbm, cot),
             (rows_hbm, rows_ref)]
        )
    ]
    feature_blocks, toks = tok.shape[:2]

    def token_copy(b):
        return pltpu.make_async_copy(
            tokens_hbm.at[:, pl.ds(pl.multiple_of(b * blk, blk), blk)], tok.at[b], tok_sem.at[b])

    blocks = lin.shape[0] // blk

    def in_turn(b):
        return lax.rem(t * blocks + b, feature_blocks)

    def token_start(b, carry):
        token_copy(in_turn(b)).start()
        return carry

    def token_wait(b, carry):
        token_copy(in_turn(b)).wait()
        return carry

    in_copies[0].start()
    lax.fori_loop(0, blocks, token_start, 0)

    neighbours = jnp.where(z > 0, 1, 0) + jnp.where(z < nz - 1, 1, 0)
    pl.semaphore_wait(barrier, nt - 1 + ny - 1 + neighbours)

    pairs = nt // 2
    pair, side = t // 2, lax.rem(t, 2)

    def lat_pair():
        return pltpu.make_async_remote_copy(
            src_ref=lpart.at[1 - side], dst_ref=lpair,
            send_sem=l0_send, recv_sem=l0_recv,
            device_id={"tensor": 2 * pair + 1 - side}, device_id_type=MESH)

    def lat_one(i):
        peer = lax.rem(pair + i, pairs)
        return pltpu.make_async_remote_copy(
            src_ref=lhalf, dst_ref=lrecv.at[i],
            send_sem=l1_send.at[i], recv_sem=l1_recv.at[i],
            device_id={"tensor": 2 * peer + side}, device_id_type=MESH)

    def lat_two(half):
        return pltpu.make_async_remote_copy(
            src_ref=lat.at[half], dst_ref=lat.at[half],
            send_sem=l2_send, recv_sem=l2_recv,
            device_id={"tensor": 2 * pair + 1 - side}, device_id_type=MESH)

    def latent_half():
        lat_pair().wait_recv()
        half = lpart[side] + lpair[...]
        lpart[side] = half
        lhalf[...] = half.astype(lhalf.dtype)
        for i in range(1, pairs):
            lat_one(i).start()

    def latent_sum():
        total = lpart[side]
        for i in range(1, pairs):
            lat_one(i).wait_recv()
            total = total + lrecv[i].astype(f32)
        lat[side] = total.astype(lat.dtype)
        lat_two(side).start()
        lax.fori_loop(blocks, feature_blocks, token_wait, 0)
        for copy in in_copies[1:]:
            copy.wait()

    def latent_done():
        lat_two(1 - side).wait_recv()

    def reach(j, cut):
        return pl.ds(pl.multiple_of(j * size + y * cut, 8), size - (ny - 1) * cut)

    def alone(j, p, cut):
        first = p * ((size - cut) // max(ny - 1, 1))
        return pl.ds(pl.multiple_of(j * size + first, 8), cut)

    def gather_copy(way, shard, j, cut, from_input=False):
        there = z + 1 if way == 0 else z - 1
        at = reach(j, cut)
        return pltpu.make_async_remote_copy(
            src_ref=panels_hbm.at[at] if from_input else pan.at[shard, at],
            dst_ref=pan.at[shard, at],
            send_sem=ag_send.at[way, shard], recv_sem=ag_recv.at[shard, j],
            device_id={"fsdp": there}, device_id_type=MESH)

    def across_copy(i, shard, j, cut):
        at = alone(j, y, cut)
        return pltpu.make_async_remote_copy(
            src_ref=pan.at[shard, at], dst_ref=pan.at[shard, at],
            send_sem=ay_send.at[shard], recv_sem=ay_recv.at[i, j],
            device_id={"dp": lax.rem(y + i, ny)}, device_id_type=MESH)

    def send_own(way, j):
        @pl.when(j < chunks)
        def _():
            by_cut(gplan, j, lambda cut: gather_copy(way, z, j, cut, True).start())

    def inside(j):
        return jnp.logical_and(j >= 0, j < chunks)

    up_ahead = jnp.where(z == 0, AHEAD_END, AHEAD)
    down_ahead = jnp.where(z == nz - 1, AHEAD_END, AHEAD)

    def first_own(j, carry):
        pl.when(jnp.logical_and(z < nz - 1, j < up_ahead))(lambda: send_own(0, j))
        pl.when(jnp.logical_and(z > 0, j < down_ahead))(lambda: send_own(1, j))
        return carry

    lax.fori_loop(0, max(AHEAD, AHEAD_END), first_own, 0)

    in_copies[0].wait()
    lax.fori_loop(0, blocks, token_wait, 0)
    lpart[...] = jnp.dot(
        jnp.concatenate([tok[t * blocks + b] for b in range(blocks)], axis=1), lin[...],
        preferred_element_type=f32,
    ).reshape(lpart.shape)

    lat_pair().start()
    lax.fori_loop(blocks, feature_blocks, token_start, 0)
    for copy in in_copies[1:]:
        copy.start()

    def front(h, tau):
        grown = lax.max(tau - GATHER_WARP - (h - 1), 0)
        return tau - (h - 1) + lax.min(grown, (nz - 1 - h) * (GATHER_LAG - 1))

    def pass_on(h, j):
        def arrived(way, shard, more):
            def act(cut):
                gather_copy(way, shard, j, cut).wait_recv()

                @pl.when(more)
                def _():
                    gather_copy(way, shard, j, cut).start()

                if cut:
                    for i in range(1, ny):
                        across_copy(i, shard, j, cut).start()

            by_cut(gplan, j, act)

        @pl.when(jnp.logical_and(inside(j), z - h >= 0))
        def _():
            arrived(0, z - h, z < nz - 1)

        @pl.when(jnp.logical_and(inside(j), z + h < nz))
        def _():
            arrived(1, z + h, z > 0)

    def across_done(j):
        def act(cut):
            if cut:
                at = pan.at[pl.ds(0, nz - 1), pl.ds(0, cut)]
                for i in range(1, ny):
                    pltpu.make_async_copy(at, at, ay_recv.at[i, j]).wait()

        by_cut(gplan, j, act)

    def column(c):
        picked = jnp.concatenate([tok[rows_ref[k, c]] for k in range(per)], axis=1)
        lines = pl.ds(pl.multiple_of(c * deep, 8), deep)
        parts = [pan[s, lines] for s in range(nz)]
        weight = jnp.concatenate(
            [parts[s][k * rows:(k + 1) * rows] for k in range(per) for s in range(nz)], axis=0)
        latent = lat[...].reshape(toks, -1)
        pre = jnp.dot(latent, lout[c], preferred_element_type=f32)
        pre = pre + jnp.dot(picked, weight, preferred_element_type=f32)
        at = pl.ds(pl.multiple_of(c * blk, blk), blk)
        square = pre * pre
        curve = jnp.tanh(GELU_SCALE * (pre + GELU_CUBIC * (square * pre)))
        half = 0.5 * (1.0 + curve)
        act_ref[:, at] = (pre * half).astype(act_ref.dtype)
        inner = GELU_SCALE * (1.0 + 3.0 * GELU_CUBIC * square)
        deriv = half + 0.5 * pre * (1.0 - curve * curve) * inner
        slope = (cot[:, at].astype(f32) * deriv).astype(jnp.bfloat16)
        grad = lax.dot_general(
            picked, slope, (((0,), (0,)), ((), ())), preferred_element_type=f32)
        for d in range(nz):
            own[d, lines] = jnp.concatenate(
                [grad[k * blk + d * rows:k * blk + (d + 1) * rows] for k in range(per)], axis=0)

    def landing(j, cut):
        return pl.ds(pl.multiple_of(j * (size // ny), 8), cut)

    def early_copy(i, j, cut):
        peer = lax.rem(y + i, ny)
        return pltpu.make_async_remote_copy(
            src_ref=xsend.at[:, alone(j, peer, cut)],
            dst_ref=xrecv.at[i - 1, :, landing(j, cut)],
            send_sem=x_send.at[i], recv_sem=x_recv.at[i, j],
            device_id={"dp": peer}, device_id_type=MESH)

    def early_start(j):
        def act(cut):
            if cut:
                for i in range(1, ny):
                    at = alone(j, lax.rem(y + i, ny), cut)
                    xsend[:, at] = own[:, at].astype(xsend.dtype)
                    early_copy(i, j, cut).start()

        by_cut(splan, j, act)

    def early_done(j):
        def act(cut):
            if cut:
                at = alone(j, y, cut)
                total = own[:, at]
                for i in range(1, ny):
                    early_copy(i, j, cut).wait_recv()
                    total = total + xrecv[i - 1, :, landing(j, cut)].astype(f32)
                own[:, at] = total

        by_cut(splan, j, act)

    def sum_copy(way, d, j, cut):
        there = z + 1 if way == 0 else z - 1
        at = reach(j, cut)
        return pltpu.make_async_remote_copy(
            src_ref=sbuf.at[d, at], dst_ref=rbuf.at[way, d, at],
            send_sem=rs_send.at[d], recv_sem=rs_recv.at[way, d, j],
            device_id={"fsdp": there}, device_id_type=MESH)

    def flow(way, d, j, first):
        def act(cut):
            at = reach(j, cut)

            @pl.when(first)
            def _():
                sbuf[d, at] = own[d, at].astype(sbuf.dtype)

            @pl.when(jnp.logical_not(first))
            def _():
                sum_copy(way, d, j, cut).wait_recv()
                sbuf[d, at] = (own[d, at] + rbuf[way, d, at].astype(f32)).astype(sbuf.dtype)

            sum_copy(way, d, j, cut).start()

        by_cut(splan, j, act)

    def final_copy(i, j, cut):
        at = reach(j, cut)
        return pltpu.make_async_remote_copy(
            src_ref=ysend.at[at], dst_ref=yrecv.at[i - 1, at],
            send_sem=y_send.at[i], recv_sem=y_recv.at[i, j],
            device_id={"dp": lax.rem(y + i, ny)}, device_id_type=MESH)

    def finish(j):
        def act(cut):
            at = reach(j, cut)

            def landed(way):
                sum_copy(way, z, j, cut).wait_recv()
                return rbuf[way, z, at].astype(f32)

            @pl.when(z == 0)
            def _():
                ysend[at] = (own[z, at] + landed(1)).astype(ysend.dtype)

            @pl.when(z == nz - 1)
            def _():
                ysend[at] = (own[z, at] + landed(0)).astype(ysend.dtype)

            @pl.when(jnp.logical_and(z > 0, z < nz - 1))
            def _():
                ysend[at] = (own[z, at] + landed(0) + landed(1)).astype(ysend.dtype)

            for i in range(1, ny):
                final_copy(i, j, cut).start()

        by_cut(splan, j, act)

    def result(j):
        def act(cut):
            for i in range(1, ny):
                peer = lax.rem(y + ny - i, ny)
                at = pl.ds(pl.multiple_of(j * size + peer * cut, 8), size - (ny - 1) * cut)
                pltpu.make_async_copy(
                    yrecv.at[i - 1, at], yrecv.at[i - 1, at], y_recv.at[i, j]).wait()
            if cut:
                mine = alone(j, y, cut)
                grad_ref[mine] = ysend[mine].astype(f32)
                for i in range(1, ny):
                    there = alone(j, lax.rem(y + ny - i, ny), cut)
                    grad_ref[there] = yrecv[i - 1, there].astype(f32)
            if size - ny * cut:
                shared = pl.ds(pl.multiple_of(j * size + (ny - 1) * cut, 8), size - ny * cut)
                value = ysend[shared].astype(f32)
                for i in range(1, ny):
                    value = value + yrecv[i - 1, shared].astype(f32)
                grad_ref[shared] = value

        by_cut(splan, j, act)

    compute_at = nz - 2 + ACROSS_LAG
    sum_at = compute_at + EARLY_LAG
    finish_at = sum_at + (nz - 1) * SUM_LAG
    steps = chunks + finish_at + FINAL_LAG

    def gathers(tau):
        def hop(k, carry):
            h = nz - 1 - k

            def each(j, carry):
                pass_on(h, j)
                return carry

            lax.fori_loop(front(h, tau), front(h, tau + 1), each, 0)
            return carry

        lax.fori_loop(0, nz - 1, hop, 0)

        def own_next(j, carry):
            pl.when(z < nz - 1)(lambda: send_own(0, j + up_ahead))
            pl.when(z > 0)(lambda: send_own(1, j + down_ahead))
            return carry

        lax.fori_loop(front(1, tau), front(1, tau + 1), own_next, 0)

    def early_front(tau):
        return tau - compute_at - 1 - lax.min(lax.max(tau - SUM_WARP, 0), EARLY_LAG - 1)

    def sums(tau):
        moved = early_front(tau) > early_front(tau - 1)
        fresh = jnp.where(moved, early_front(tau), -1)
        pl.when(inside(fresh))(lambda: early_done(fresh))
        summed = tau - sum_at
        up = jnp.where(z == 0, fresh, summed - z * SUM_LAG)
        down = jnp.where(z == nz - 1, fresh, summed - (nz - 1 - z) * SUM_LAG)

        def towards(d, carry):
            far = nz - 1 - d

            @pl.when(jnp.logical_and(far > z, inside(up)))
            def _():
                flow(0, far, up, z == 0)

            @pl.when(jnp.logical_and(d < z, inside(down)))
            def _():
                flow(1, d, down, z == nz - 1)

            return carry

        lax.fori_loop(0, nz, towards, 0)
        last = tau - finish_at
        pl.when(inside(last))(lambda: finish(last))
        done = last - FINAL_LAG
        pl.when(inside(done))(lambda: result(done))

    def latents(tau):
        pl.when(tau == 0)(latent_half)
        pl.when(tau == 1)(latent_sum)
        pl.when(tau == compute_at)(latent_done)

    def columns(tau):
        now = tau - compute_at

        @pl.when(inside(now))
        def _():
            across_done(now)
            for i in range(nc):
                column(now * nc + i)
            early_start(now)

    stages = {"g": gathers, "s": sums, "l": latents, "r": columns}

    def step(tau, carry):
        for name in ORDER:
            stages[name](tau)
        return carry

    lax.fori_loop(0, steps, step, 0)

    lat_pair().wait_send()
    for i in range(1, pairs):
        lat_one(i).wait_send()
    lat_two(side).wait_send()

    def gather_left(way, s):
        at = pan.at[s, pl.ds(0, gwide)]
        pltpu.make_async_copy(at, at, ag_send.at[way, s]).wait()

    def left(s, carry):
        @pl.when(jnp.logical_and(s <= z, z < nz - 1))
        def _():
            gather_left(0, s)

        @pl.when(jnp.logical_and(s >= z, z > 0))
        def _():
            gather_left(1, s)

        @pl.when(s != z)
        def _():
            if gcuts:
                at = pan.at[s, pl.ds(0, gcuts)]
                for i in range(1, ny):
                    pltpu.make_async_copy(at, at, ay_send.at[s]).wait()
            at = sbuf.at[s, pl.ds(0, swide)]
            pltpu.make_async_copy(at, at, rs_send.at[s]).wait()

        return carry

    lax.fori_loop(0, nz, left, 0)
    for i in range(1, ny):
        at = ysend.at[pl.ds(0, swide)]
        pltpu.make_async_copy(at, at, y_send.at[i]).wait()
        if scuts:
            at = xsend.at[:, pl.ds(0, scuts)]
            pltpu.make_async_copy(at, at, x_send.at[i]).wait()


def write_out(act_in, grad_in, act_out, grad_out, sem):
    copies = []
    for a, (src, dst) in enumerate([(act_in, act_out), (grad_in, grad_out)]):
        step = src.shape[0] // PIECES
        for i in range(PIECES):
            at = pl.ds(i * step, step)
            copies.append(pltpu.make_async_copy(src.at[at], dst.at[at], sem.at[a, i]))
    for copy in copies:
        copy.start()
    for copy in copies:
        copy.wait()


def on_device(sizes, tokens, panels, block_rows, low_in, low_out, cotangent):
    nz, ny, nt = sizes
    cols, per, rows, blk = panels.shape
    toks, rank = tokens.shape[0], low_in.shape[1]
    nc = COLS if ny <= 2 and cols % COLS == 0 else 4 if cols % 4 == 0 else 1
    chunks = cols // nc
    size = nc * per * rows

    def plan_of(cuts):
        if ny != 2:
            return ((0, chunks, 0 if ny == 1 else size // ny),)
        plan, first = [], 0
        for end, cut in cuts:
            end = end * chunks // 14
            if end > first:
                plan.append((first, end, size * cut // 16 // 16 * 16))
            first = max(first, end)
        return tuple(plan)

    bf16, f32 = jnp.bfloat16, jnp.float32
    hop_type = bf16 if nz <= 4 and ny <= 2 else f32
    low_out = low_out.reshape(cols, rank, blk)
    lines = panels.reshape(cols * per * rows, blk)
    height = lines.shape[0]
    hbm = pl.BlockSpec(memory_space=pl.ANY)
    vmem = pl.BlockSpec(memory_space=pltpu.VMEM)
    dma = pltpu.SemaphoreType.DMA
    others = max(ny - 1, 1)
    activated, grad = pl.pallas_call(
        functools.partial(
            kernel, nz, ny, nt, per, rows, size, plan_of(GATHER_CUT), plan_of(SUM_CUT)),
        out_shape=(
            pltpu.VMEM(cotangent.shape, bf16),
            pltpu.VMEM(lines.shape, f32),
        ),
        in_specs=[hbm] * 6,
        out_specs=(vmem, vmem),
        scratch_shapes=[
            pltpu.SMEM((per, cols), jnp.int32),
            pltpu.VMEM((tokens.shape[1] // blk, toks, blk), bf16),
            pltpu.VMEM(low_in.shape, bf16),
            pltpu.VMEM(low_out.shape, bf16),
            pltpu.VMEM(cotangent.shape, bf16),
            pltpu.VMEM((nz, height, blk), bf16),
            pltpu.VMEM((nz, height, blk), f32),
            pltpu.VMEM((nz, height, blk), hop_type),
            pltpu.VMEM((2, nz, height, blk), hop_type),
            pltpu.VMEM((height, blk), hop_type),
            pltpu.VMEM((others, height, blk), hop_type),
            pltpu.VMEM((nz, height, blk), hop_type),
            pltpu.VMEM((others, nz, height // ny, blk), hop_type),
            pltpu.VMEM((2, toks // 2, rank), f32),
            pltpu.VMEM((toks // 2, rank), f32),
            pltpu.VMEM((toks // 2, rank), f32),
            pltpu.VMEM((nt // 2, toks // 2, rank), f32),
            pltpu.VMEM((2, toks // 2, rank), bf16),
            dma((5,)),
            dma((tokens.shape[1] // blk,)),
            dma((2, nz)),
            dma((nz, chunks)),
            dma((nz,)),
            dma((ny, chunks)),
            dma((nz,)),
            dma((2, nz, chunks)),
            dma((ny,)),
            dma((ny, chunks)),
            dma((ny,)),
            dma((ny, chunks)),
            dma,
            dma,
            dma((nt,)),
            dma((nt,)),
            dma,
            dma,
        ],
        compiler_params=pltpu.CompilerParams(
            collective_id=0, has_side_effects=True, vmem_limit_bytes=52 * 1024 * 1024),
    )(tokens, lines, block_rows.T, low_in, low_out, cotangent)
    activated, grad = pl.pallas_call(
        write_out,
        out_shape=(
            jax.ShapeDtypeStruct(cotangent.shape, bf16),
            jax.ShapeDtypeStruct(lines.shape, f32),
        ),
        in_specs=[vmem, vmem],
        out_specs=(hbm, hbm),
        scratch_shapes=[dma((2, PIECES))],
        compiler_params=pltpu.CompilerParams(vmem_limit_bytes=1024 * 1024),
    )(pltpu.with_memory_space_constraint(activated, pltpu.VMEM), pltpu.with_memory_space_constraint(grad, pltpu.VMEM))
    return activated, grad.reshape(panels.shape)


def solution(mesh):
    in_specs = (
        P(("fsdp", "dp"), None),
        P("tensor", None, "fsdp", None),
        P("tensor", None),
        P("tensor", None),
        P("tensor", None, None, None),
        P(("fsdp", "dp"), "tensor"),
    )
    out_specs = (P(("fsdp", "dp"), "tensor"), P("tensor", None, "fsdp", None))
    sizes = tuple(mesh.shape[name] for name in ("fsdp", "dp", "tensor"))
    return jax.shard_map(
        functools.partial(on_device, sizes),
        mesh=mesh, in_specs=in_specs, out_specs=out_specs, check_vma=False,
    )
```

```python
import functools
import math

import jax
import jax.numpy as jnp
from jax import lax
from jax.experimental import pallas as pl
from jax.experimental.pallas import tpu as pltpu
from jax.sharding import PartitionSpec as P

MESH = pl.DeviceIdType.MESH
GELU_SCALE = math.sqrt(2.0 / math.pi)
GELU_CUBIC = 0.044715
COLS = 2
AHEAD = 4
AHEAD_END = 14
GATHER_LAG = 2
ACROSS_LAG = 1
EARLY_LAG = 2
SUM_LAG = 4
FINAL_LAG = 4
GATHER_CUT = ((5, 8), (11, 5), (14, 0))
SUM_CUT = ((3, 1), (10, 5), (14, 7))
PIECES = 1
GATHER_WARP = 0
SUM_WARP = 6
ORDER = "glrs"


def by_cut(plan, j, act):
    if len(plan) == 1:
        act(plan[0][2])
    else:
        for first, end, cut in plan:
            pl.when(jnp.logical_and(j >= first, j < end))(functools.partial(act, cut))


def kernel(
    nz, ny, nt, per, rows, size, gplan, splan,
    tokens_hbm, panels_hbm, rows_hbm, low_in_hbm, low_out_hbm, cot_hbm,
    act_ref, grad_ref,
    rows_ref, tok, lin, lout, cot, pan, own, sbuf, rbuf, ysend, yrecv, xsend, xrecv,
    lpart, lpair, lhalf, lrecv, lat,
    local_sem, tok_sem, ag_send, ag_recv, ay_send, ay_recv, rs_send, rs_recv,
    y_send, y_recv, x_send, x_recv, l0_send, l0_recv, l1_send, l1_recv, l2_send, l2_recv,
):
    z, y, t = lax.axis_index("fsdp"), lax.axis_index("dp"), lax.axis_index("tensor")
    height, blk = panels_hbm.shape
    chunks = height // size
    deep = per * rows
    nc = size // deep
    gcuts, scuts = (
        sum((end - first) * cut for first, end, cut in plan) for plan in (gplan, splan))
    gwide, swide = height - (ny - 1) * gcuts, height - (ny - 1) * scuts
    f32 = jnp.float32

    barrier = pltpu.get_barrier_semaphore()

    @pl.when(z > 0)
    def _():
        pl.semaphore_signal(barrier, inc=1, device_id={"fsdp": z - 1}, device_id_type=MESH)

    @pl.when(z < nz - 1)
    def _():
        pl.semaphore_signal(barrier, inc=1, device_id={"fsdp": z + 1}, device_id_type=MESH)

    for i in range(1, nt):
        pl.semaphore_signal(
            barrier, inc=1, device_id={"tensor": lax.rem(t + i, nt)}, device_id_type=MESH)
    for i in range(1, ny):
        pl.semaphore_signal(
            barrier, inc=1, device_id={"dp": lax.rem(y + i, ny)}, device_id_type=MESH)

    in_copies = [
        pltpu.make_async_copy(src, dst, local_sem.at[i])
        for i, (src, dst) in enumerate(
            [(low_in_hbm, lin), (panels_hbm, pan.at[z]), (low_out_hbm, lout), (cot_hbm, cot),
             (rows_hbm, rows_ref)]
        )
    ]
    feature_blocks, toks = tok.shape[:2]

    def token_copy(b):
        return pltpu.make_async_copy(
            tokens_hbm.at[:, pl.ds(pl.multiple_of(b * blk, blk), blk)], tok.at[b], tok_sem.at[b])

    blocks = lin.shape[0] // blk

    def in_turn(b):
        return lax.rem(t * blocks + b, feature_blocks)

    def token_start(b, carry):
        token_copy(in_turn(b)).start()
        return carry

    def token_wait(b, carry):
        token_copy(in_turn(b)).wait()
        return carry

    in_copies[0].start()
    lax.fori_loop(0, blocks, token_start, 0)

    neighbours = jnp.where(z > 0, 1, 0) + jnp.where(z < nz - 1, 1, 0)
    pl.semaphore_wait(barrier, nt - 1 + ny - 1 + neighbours)

    pairs = nt // 2
    pair, side = t // 2, lax.rem(t, 2)

    def lat_pair():
        return pltpu.make_async_remote_copy(
            src_ref=lpart.at[1 - side], dst_ref=lpair,
            send_sem=l0_send, recv_sem=l0_recv,
            device_id={"tensor": 2 * pair + 1 - side}, device_id_type=MESH)

    def lat_one(i):
        peer = lax.rem(pair + i, pairs)
        return pltpu.make_async_remote_copy(
            src_ref=lhalf, dst_ref=lrecv.at[i],
            send_sem=l1_send.at[i], recv_sem=l1_recv.at[i],
            device_id={"tensor": 2 * peer + side}, device_id_type=MESH)

    def lat_two(half):
        return pltpu.make_async_remote_copy(
            src_ref=lat.at[half], dst_ref=lat.at[half],
            send_sem=l2_send, recv_sem=l2_recv,
            device_id={"tensor": 2 * pair + 1 - side}, device_id_type=MESH)

    def latent_half():
        lat_pair().wait_recv()
        half = lpart[side] + lpair[...]
        lpart[side] = half
        lhalf[...] = half.astype(lhalf.dtype)
        for i in range(1, pairs):
            lat_one(i).start()

    def latent_sum():
        total = lpart[side]
        for i in range(1, pairs):
            lat_one(i).wait_recv()
            total = total + lrecv[i].astype(f32)
        lat[side] = total.astype(lat.dtype)
        lat_two(side).start()
        lax.fori_loop(blocks, feature_blocks, token_wait, 0)
        for copy in in_copies[1:]:
            copy.wait()

    def latent_done():
        lat_two(1 - side).wait_recv()

    def reach(j, cut):
        return pl.ds(pl.multiple_of(j * size + y * cut, 8), size - (ny - 1) * cut)

    def alone(j, p, cut):
        first = p * ((size - cut) // max(ny - 1, 1))
        return pl.ds(pl.multiple_of(j * size + first, 8), cut)

    def gather_copy(way, shard, j, cut, from_input=False):
        there = z + 1 if way == 0 else z - 1
        at = reach(j, cut)
        return pltpu.make_async_remote_copy(
            src_ref=panels_hbm.at[at] if from_input else pan.at[shard, at],
            dst_ref=pan.at[shard, at],
            send_sem=ag_send.at[way, shard], recv_sem=ag_recv.at[shard, j],
            device_id={"fsdp": there}, device_id_type=MESH)

    def across_copy(i, shard, j, cut):
        at = alone(j, y, cut)
        return pltpu.make_async_remote_copy(
            src_ref=pan.at[shard, at], dst_ref=pan.at[shard, at],
            send_sem=ay_send.at[shard], recv_sem=ay_recv.at[i, j],
            device_id={"dp": lax.rem(y + i, ny)}, device_id_type=MESH)

    def send_own(way, j):
        @pl.when(j < chunks)
        def _():
            by_cut(gplan, j, lambda cut: gather_copy(way, z, j, cut, True).start())

    def inside(j):
        return jnp.logical_and(j >= 0, j < chunks)

    up_ahead = jnp.where(z == 0, AHEAD_END, AHEAD)
    down_ahead = jnp.where(z == nz - 1, AHEAD_END, AHEAD)

    def first_own(j, carry):
        pl.when(jnp.logical_and(z < nz - 1, j < up_ahead))(lambda: send_own(0, j))
        pl.when(jnp.logical_and(z > 0, j < down_ahead))(lambda: send_own(1, j))
        return carry

    lax.fori_loop(0, max(AHEAD, AHEAD_END), first_own, 0)

    in_copies[0].wait()
    lax.fori_loop(0, blocks, token_wait, 0)
    lpart[...] = jnp.dot(
        jnp.concatenate([tok[t * blocks + b] for b in range(blocks)], axis=1), lin[...],
        preferred_element_type=f32,
    ).reshape(lpart.shape)

    lat_pair().start()
    lax.fori_loop(blocks, feature_blocks, token_start, 0)
    for copy in in_copies[1:]:
        copy.start()

    def front(h, tau):
        grown = lax.max(tau - GATHER_WARP - (h - 1), 0)
        return tau - (h - 1) + lax.min(grown, (nz - 1 - h) * (GATHER_LAG - 1))

    def pass_on(h, j):
        def arrived(way, shard, more):
            def act(cut):
                gather_copy(way, shard, j, cut).wait_recv()

                @pl.when(more)
                def _():
                    gather_copy(way, shard, j, cut).start()

                if cut:
                    for i in range(1, ny):
                        across_copy(i, shard, j, cut).start()

            by_cut(gplan, j, act)

        @pl.when(jnp.logical_and(inside(j), z - h >= 0))
        def _():
            arrived(0, z - h, z < nz - 1)

        @pl.when(jnp.logical_and(inside(j), z + h < nz))
        def _():
            arrived(1, z + h, z > 0)

    def across_done(j):
        def act(cut):
            if cut:
                at = pan.at[pl.ds(0, nz - 1), pl.ds(0, cut)]
                for i in range(1, ny):
                    pltpu.make_async_copy(at, at, ay_recv.at[i, j]).wait()

        by_cut(gplan, j, act)

    def column(c):
        picked = jnp.concatenate([tok[rows_ref[k, c]] for k in range(per)], axis=1)
        lines = pl.ds(pl.multiple_of(c * deep, 8), deep)
        parts = [pan[s, lines] for s in range(nz)]
        weight = jnp.concatenate(
            [parts[s][k * rows:(k + 1) * rows] for k in range(per) for s in range(nz)], axis=0)
        latent = lat[...].reshape(toks, -1)
        pre = jnp.dot(latent, lout[c], preferred_element_type=f32)
        pre = pre + jnp.dot(picked, weight, preferred_element_type=f32)
        at = pl.ds(pl.multiple_of(c * blk, blk), blk)
        square = pre * pre
        curve = jnp.tanh(GELU_SCALE * (pre + GELU_CUBIC * (square * pre)))
        half = 0.5 * (1.0 + curve)
        act_ref[:, at] = (pre * half).astype(act_ref.dtype)
        inner = GELU_SCALE * (1.0 + 3.0 * GELU_CUBIC * square)
        deriv = half + 0.5 * pre * (1.0 - curve * curve) * inner
        slope = (cot[:, at].astype(f32) * deriv).astype(jnp.bfloat16)
        grad = lax.dot_general(
            picked, slope, (((0,), (0,)), ((), ())), preferred_element_type=f32)
        for d in range(nz):
            own[d, lines] = jnp.concatenate(
                [grad[k * blk + d * rows:k * blk + (d + 1) * rows] for k in range(per)], axis=0)

    def landing(j, cut):
        return pl.ds(pl.multiple_of(j * (size // ny), 8), cut)

    def early_copy(i, j, cut):
        peer = lax.rem(y + i, ny)
        return pltpu.make_async_remote_copy(
            src_ref=xsend.at[:, alone(j, peer, cut)],
            dst_ref=xrecv.at[i - 1, :, landing(j, cut)],
            send_sem=x_send.at[i], recv_sem=x_recv.at[i, j],
            device_id={"dp": peer}, device_id_type=MESH)

    def early_start(j):
        def act(cut):
            if cut:
                for i in range(1, ny):
                    at = alone(j, lax.rem(y + i, ny), cut)
                    xsend[:, at] = own[:, at].astype(xsend.dtype)
                    early_copy(i, j, cut).start()

        by_cut(splan, j, act)

    def early_done(j):
        def act(cut):
            if cut:
                at = alone(j, y, cut)
                total = own[:, at]
                for i in range(1, ny):
                    early_copy(i, j, cut).wait_recv()
                    total = total + xrecv[i - 1, :, landing(j, cut)].astype(f32)
                own[:, at] = total

        by_cut(splan, j, act)

    def sum_copy(way, d, j, cut):
        there = z + 1 if way == 0 else z - 1
        at = reach(j, cut)
        return pltpu.make_async_remote_copy(
            src_ref=sbuf.at[d, at], dst_ref=rbuf.at[way, d, at],
            send_sem=rs_send.at[d], recv_sem=rs_recv.at[way, d, j],
            device_id={"fsdp": there}, device_id_type=MESH)

    def flow(way, d, j, first):
        def act(cut):
            at = reach(j, cut)

            @pl.when(first)
            def _():
                sbuf[d, at] = own[d, at].astype(sbuf.dtype)

            @pl.when(jnp.logical_not(first))
            def _():
                sum_copy(way, d, j, cut).wait_recv()
                sbuf[d, at] = (own[d, at] + rbuf[way, d, at].astype(f32)).astype(sbuf.dtype)

            sum_copy(way, d, j, cut).start()

        by_cut(splan, j, act)

    def final_copy(i, j, cut):
        at = reach(j, cut)
        return pltpu.make_async_remote_copy(
            src_ref=ysend.at[at], dst_ref=yrecv.at[i - 1, at],
            send_sem=y_send.at[i], recv_sem=y_recv.at[i, j],
            device_id={"dp": lax.rem(y + i, ny)}, device_id_type=MESH)

    def finish(j):
        def act(cut):
            at = reach(j, cut)

            def landed(way):
                sum_copy(way, z, j, cut).wait_recv()
                return rbuf[way, z, at].astype(f32)

            @pl.when(z == 0)
            def _():
                ysend[at] = (own[z, at] + landed(1)).astype(ysend.dtype)

            @pl.when(z == nz - 1)
            def _():
                ysend[at] = (own[z, at] + landed(0)).astype(ysend.dtype)

            @pl.when(jnp.logical_and(z > 0, z < nz - 1))
            def _():
                ysend[at] = (own[z, at] + landed(0) + landed(1)).astype(ysend.dtype)

            for i in range(1, ny):
                final_copy(i, j, cut).start()

        by_cut(splan, j, act)

    def result(j):
        def act(cut):
            for i in range(1, ny):
                peer = lax.rem(y + ny - i, ny)
                at = pl.ds(pl.multiple_of(j * size + peer * cut, 8), size - (ny - 1) * cut)
                pltpu.make_async_copy(
                    yrecv.at[i - 1, at], yrecv.at[i - 1, at], y_recv.at[i, j]).wait()
            if cut:
                mine = alone(j, y, cut)
                grad_ref[mine] = ysend[mine].astype(f32)
                for i in range(1, ny):
                    there = alone(j, lax.rem(y + ny - i, ny), cut)
                    grad_ref[there] = yrecv[i - 1, there].astype(f32)
            if size - ny * cut:
                shared = pl.ds(pl.multiple_of(j * size + (ny - 1) * cut, 8), size - ny * cut)
                value = ysend[shared].astype(f32)
                for i in range(1, ny):
                    value = value + yrecv[i - 1, shared].astype(f32)
                grad_ref[shared] = value

        by_cut(splan, j, act)

    compute_at = nz - 2 + ACROSS_LAG
    sum_at = compute_at + EARLY_LAG
    finish_at = sum_at + (nz - 1) * SUM_LAG
    steps = chunks + finish_at + FINAL_LAG

    def gathers(tau):
        def hop(k, carry):
            h = nz - 1 - k

            def each(j, carry):
                pass_on(h, j)
                return carry

            lax.fori_loop(front(h, tau), front(h, tau + 1), each, 0)
            return carry

        lax.fori_loop(0, nz - 1, hop, 0)

        def own_next(j, carry):
            pl.when(z < nz - 1)(lambda: send_own(0, j + up_ahead))
            pl.when(z > 0)(lambda: send_own(1, j + down_ahead))
            return carry

        lax.fori_loop(front(1, tau), front(1, tau + 1), own_next, 0)

    def early_front(tau):
        return tau - compute_at - 1 - lax.min(lax.max(tau - SUM_WARP, 0), EARLY_LAG - 1)

    def sums(tau):
        moved = early_front(tau) > early_front(tau - 1)
        fresh = jnp.where(moved, early_front(tau), -1)
        pl.when(inside(fresh))(lambda: early_done(fresh))
        summed = tau - sum_at
        up = jnp.where(z == 0, fresh, summed - z * SUM_LAG)
        down = jnp.where(z == nz - 1, fresh, summed - (nz - 1 - z) * SUM_LAG)

        def towards(d, carry):
            far = nz - 1 - d

            @pl.when(jnp.logical_and(far > z, inside(up)))
            def _():
                flow(0, far, up, z == 0)

            @pl.when(jnp.logical_and(d < z, inside(down)))
            def _():
                flow(1, d, down, z == nz - 1)

            return carry

        lax.fori_loop(0, nz, towards, 0)
        last = tau - finish_at
        pl.when(inside(last))(lambda: finish(last))
        done = last - FINAL_LAG
        pl.when(inside(done))(lambda: result(done))

    def latents(tau):
        pl.when(tau == 0)(latent_half)
        pl.when(tau == 1)(latent_sum)
        pl.when(tau == compute_at)(latent_done)

    def columns(tau):
        now = tau - compute_at

        @pl.when(inside(now))
        def _():
            across_done(now)
            for i in range(nc):
                column(now * nc + i)
            early_start(now)

    stages = {"g": gathers, "s": sums, "l": latents, "r": columns}

    def step(tau, carry):
        for name in ORDER:
            stages[name](tau)
        return carry

    lax.fori_loop(0, steps, step, 0)

    lat_pair().wait_send()
    for i in range(1, pairs):
        lat_one(i).wait_send()
    lat_two(side).wait_send()

    def gather_left(way, s):
        at = pan.at[s, pl.ds(0, gwide)]
        pltpu.make_async_copy(at, at, ag_send.at[way, s]).wait()

    def left(s, carry):
        @pl.when(jnp.logical_and(s <= z, z < nz - 1))
        def _():
            gather_left(0, s)

        @pl.when(jnp.logical_and(s >= z, z > 0))
        def _():
            gather_left(1, s)

        @pl.when(s != z)
        def _():
            if gcuts:
                at = pan.at[s, pl.ds(0, gcuts)]
                for i in range(1, ny):
                    pltpu.make_async_copy(at, at, ay_send.at[s]).wait()
            at = sbuf.at[s, pl.ds(0, swide)]
            pltpu.make_async_copy(at, at, rs_send.at[s]).wait()

        return carry

    lax.fori_loop(0, nz, left, 0)
    for i in range(1, ny):
        at = ysend.at[pl.ds(0, swide)]
        pltpu.make_async_copy(at, at, y_send.at[i]).wait()
        if scuts:
            at = xsend.at[:, pl.ds(0, scuts)]
            pltpu.make_async_copy(at, at, x_send.at[i]).wait()


def write_out(act_in, grad_in, act_out, grad_out, sem):
    copies = []
    for a, (src, dst) in enumerate([(act_in, act_out), (grad_in, grad_out)]):
        step = src.shape[0] // PIECES
        for i in range(PIECES):
            at = pl.ds(i * step, step)
            copies.append(pltpu.make_async_copy(src.at[at], dst.at[at], sem.at[a, i]))
    for copy in copies:
        copy.start()
    for copy in copies:
        copy.wait()


def on_device(sizes, tokens, panels, block_rows, low_in, low_out, cotangent):
    nz, ny, nt = sizes
    cols, per, rows, blk = panels.shape
    toks, rank = tokens.shape[0], low_in.shape[1]
    nc = COLS if ny <= 2 and cols % COLS == 0 else 4 if cols % 4 == 0 else 1
    chunks = cols // nc
    size = nc * per * rows

    def plan_of(cuts):
        if ny != 2:
            return ((0, chunks, 0 if ny == 1 else size // ny),)
        plan, first = [], 0
        for end, cut in cuts:
            end = end * chunks // 14
            if end > first:
                plan.append((first, end, size * cut // 16 // 16 * 16))
            first = max(first, end)
        return tuple(plan)

    bf16, f32 = jnp.bfloat16, jnp.float32
    hop_type = bf16 if nz <= 4 and ny <= 2 else f32
    low_out = low_out.reshape(cols, rank, blk)
    lines = panels.reshape(cols * per * rows, blk)
    height = lines.shape[0]
    hbm = pl.BlockSpec(memory_space=pl.ANY)
    vmem = pl.BlockSpec(memory_space=pltpu.VMEM)
    dma = pltpu.SemaphoreType.DMA
    others = max(ny - 1, 1)
    activated, grad = pl.pallas_call(
        functools.partial(
            kernel, nz, ny, nt, per, rows, size, plan_of(GATHER_CUT), plan_of(SUM_CUT)),
        out_shape=(
            pltpu.VMEM(cotangent.shape, bf16),
            pltpu.VMEM(lines.shape, f32),
        ),
        in_specs=[hbm] * 6,
        out_specs=(vmem, vmem),
        scratch_shapes=[
            pltpu.SMEM((per, cols), jnp.int32),
            pltpu.VMEM((tokens.shape[1] // blk, toks, blk), bf16),
            pltpu.VMEM(low_in.shape, bf16),
            pltpu.VMEM(low_out.shape, bf16),
            pltpu.VMEM(cotangent.shape, bf16),
            pltpu.VMEM((nz, height, blk), bf16),
            pltpu.VMEM((nz, height, blk), f32),
            pltpu.VMEM((nz, height, blk), hop_type),
            pltpu.VMEM((2, nz, height, blk), hop_type),
            pltpu.VMEM((height, blk), hop_type),
            pltpu.VMEM((others, height, blk), hop_type),
            pltpu.VMEM((nz, height, blk), hop_type),
            pltpu.VMEM((others, nz, height // ny, blk), hop_type),
            pltpu.VMEM((2, toks // 2, rank), f32),
            pltpu.VMEM((toks // 2, rank), f32),
            pltpu.VMEM((toks // 2, rank), f32),
            pltpu.VMEM((nt // 2, toks // 2, rank), f32),
            pltpu.VMEM((2, toks // 2, rank), bf16),
            dma((5,)),
            dma((tokens.shape[1] // blk,)),
            dma((2, nz)),
            dma((nz, chunks)),
            dma((nz,)),
            dma((ny, chunks)),
            dma((nz,)),
            dma((2, nz, chunks)),
            dma((ny,)),
            dma((ny, chunks)),
            dma((ny,)),
            dma((ny, chunks)),
            dma,
            dma,
            dma((nt,)),
            dma((nt,)),
            dma,
            dma,
        ],
        compiler_params=pltpu.CompilerParams(
            collective_id=0, has_side_effects=True, vmem_limit_bytes=52 * 1024 * 1024),
    )(tokens, lines, block_rows.T, low_in, low_out, cotangent)
    activated, grad = pl.pallas_call(
        write_out,
        out_shape=(
            jax.ShapeDtypeStruct(cotangent.shape, bf16),
            jax.ShapeDtypeStruct(lines.shape, f32),
        ),
        in_specs=[vmem, vmem],
        out_specs=(hbm, hbm),
        scratch_shapes=[dma((2, PIECES))],
        compiler_params=pltpu.CompilerParams(vmem_limit_bytes=1024 * 1024),
    )(pltpu.with_memory_space_constraint(activated, pltpu.VMEM), pltpu.with_memory_space_constraint(grad, pltpu.VMEM))
    return activated, grad.reshape(panels.shape)


def solution(mesh):
    in_specs = (
        P(("fsdp", "dp"), None),
        P("tensor", None, "fsdp", None),
        P("tensor", None),
        P("tensor", None),
        P("tensor", None, None, None),
        P(("fsdp", "dp"), "tensor"),
    )
    out_specs = (P(("fsdp", "dp"), "tensor"), P("tensor", None, "fsdp", None))
    sizes = tuple(mesh.shape[name] for name in ("fsdp", "dp", "tensor"))
    return jax.shard_map(
        functools.partial(on_device, sizes),
        mesh=mesh, in_specs=in_specs, out_specs=out_specs, check_vma=False,
    )
```
